512 devices in a mesh: inst: 16 (over y_lo, x, core), sector: 32 (over y_hi, z).
Axes of the slice: x: 4, y: 4 (y_hi: 2, y_lo: 2; y = y_hi * 2 + y_lo), z: 16, core: 2. Of those that a mesh axis runs over, the one named last changes fastest.
Arguments:
- lam_init: float32 [16, 512, 32, 128], P('inst', 'sector'), may hold values from -6 to 6
- rhs: float32 [16, 512, 32, 128], P('inst', 'sector'), may hold values from -6 to 6
- relax: float32 [16, 512, 128], P('inst', 'sector'), may hold values from 0.15 to 0.6
- cond: float32 [512, 128], P('sector'), may hold values from 0.05 to 0.4
- jac: bfloat16 [16, 512, 6, 128, 128], P('inst', 'sector'), may hold values from -0.21875 to 0.21875
- rotor_jac: bfloat16 [16, 128, 128, 128], P('inst', 'sector'), may hold values from -0.5 to 0.5
- cols: int32 [512, 6], P('sector'), may hold values from 0 to 17
- rotor_shift: int32 [16, 128], P('inst', 'sector'), may hold values from 0 to 1
- owned: int32 [32], P('sector'), may hold values from 1 to 12, 288 in all
Outputs:
- adjoint: float32 [16, 512, 32, 128], P('inst', 'sector')
The draws below stay inside these ranges and needn't reach their ends.
All inputs are finite; a program needn't handle non-finite values. No bound on the sum of `owned` on one device may be relied on, other than what follows from the above.
Results may differ from the reference program's by a relative error of at most 0.002.
Values may be sent and summed in bfloat16 or wider, within the bound.
No kernel may reach another device: no remote copies, remote signals or barrier semaphores. Data moves between devices by JAX's collectives and lax.ppermute only.
A program may use at most 64 MiB of HBM per device.

```python
import math
import jax
import jax.numpy as jnp
import numpy as np
from jax import lax

NT = 16
BS = 128
K = 6
NB = 16
NR = 4
R = 32
SWEEPS = 2
SECTORS = 32
N_SECTOR = 32


def plant(entries, key, smallest, largest):
    shape = entries.shape
    place = [jax.random.randint(jax.random.fold_in(key, axis), (), 0, shape[axis]) for axis in range(len(shape))]
    entries = entries.at[tuple(place)].set(smallest)
    longest = shape.index(max(shape))
    place[longest] = (place[longest] + 1) % shape[longest]
    return entries.at[tuple(place)].set(largest)


def block_scale(key, extent, split, low, high):
    gain, own = 1.0, jax.random.fold_in(key, 6)
    for position, parts in split:
        heights = jnp.exp(jax.random.uniform(jax.random.fold_in(own, position), (parts,), jnp.float32, low / len(split), high / len(split)))
        gain = gain * jnp.repeat(heights, extent[position] // parts).reshape([-1 if axis == position else 1 for axis in range(len(extent))])
    return gain


def length_profile(number_of, total, limit, slope):
    weights = [(1 << 20) // math.isqrt(standing ** slope) + 1 for standing in range(2, number_of + 1)]
    spare, given = total - limit - (number_of - 1), [1] * (number_of - 1)
    while spare > 0:
        free = [i for i in range(number_of - 1) if given[i] < limit]
        mass, left = sum([weights[i] for i in free]), spare
        for i in free:
            more = min(limit - given[i], max(1, left * weights[i] // mass), spare)
            given[i] = given[i] + more
            spare = spare - more
    return np.array([limit] + given)


def uneven_parts(own_key, amount, total, most, lean):
    if amount == 2:
        one = jax.random.randint(own_key, (), max(1, total - most), min(most, total - 1) + 1)
        return jnp.stack([one, total - one])
    sizes = jnp.asarray(length_profile(amount, total, most, lean), jnp.int32)
    couples = (amount - 1) // 2
    source_of, sink = sizes[1:1 + 2 * couples:2], sizes[2:2 + 2 * couples:2]
    room = jnp.minimum(source_of - 1, most - sink)
    shifted = jax.random.randint(jax.random.fold_in(own_key, 1), (couples,), 0, 1 << 20) % (room + 1)
    sizes = sizes.at[1:1 + 2 * couples:2].set(source_of - shifted).at[2:2 + 2 * couples:2].set(sink + shifted)
    return sizes[jax.random.permutation(jax.random.fold_in(own_key, 2), amount)]


def gaussian(key, dims, deviation, limit, split=(), dtype=jnp.bfloat16):
    entries = deviation * jax.random.normal(key, dims, jnp.float32)
    if split:
        entries = entries * block_scale(key, dims, split, -0.22, 0.18)
    return jnp.clip(entries, -limit, limit).astype(dtype)


def setup_inputs(seed: int = 0) -> dict:
    seeds = jax.random.split(jax.random.key(seed), 10)
    return {
        "lam_init": gaussian(seeds[0], (NT, SECTORS * NB, R, BS), 1.0, 6.0, ((0, 16), (1, 32)), jnp.float32),
        "rhs": gaussian(seeds[1], (NT, SECTORS * NB, R, BS), 1.0, 6.0, ((0, 16), (1, 32)), jnp.float32),
        "relax": jnp.clip(jnp.exp(math.log(0.6) - 1.3862944 * jax.random.uniform(seeds[2], (NT, SECTORS * NB, BS), jnp.float32) ** block_scale(seeds[2], (NT, SECTORS * NB, BS), ((0, 16), (1, 32)), -0.2, 0.2)), 0.15, 0.6),
        "cond": jnp.clip(jnp.exp(math.log(0.4) - 2.0794415 * jax.random.uniform(seeds[3], (SECTORS * NB, BS), jnp.float32) ** block_scale(seeds[3], (SECTORS * NB, BS), ((0, 32),), -0.2, 0.2)), 0.05, 0.4),
        "jac": gaussian(seeds[4], (NT, SECTORS * NB, K, BS, BS), (K * BS) ** -0.5, 0.21875, ((0, 16), (1, 32))),
        "rotor_jac": gaussian(seeds[5], (NT, SECTORS * NR, BS, BS), BS ** -0.5, 0.5, ((0, 16), (1, 32))),
        "cols": plant(jax.random.randint(seeds[6], (SECTORS * NB, K), 0, NB + 2), jax.random.fold_in(seeds[6], 1), 0, (NB + 2) - 1).astype(jnp.int32),
        "rotor_shift": plant(jax.random.randint(seeds[7], (NT, SECTORS * NR), 0, 2), jax.random.fold_in(seeds[7], 1), 0, 1).astype(jnp.int32),
        "owned": uneven_parts(seeds[8], SECTORS, N_SECTOR * (NB - NR) * 3 // 4, NB - NR, 2).astype(jnp.int32),
    }


def spectral_matrix():
    index = jnp.arange(NT)
    offset = index[:, None] - index[None, :]
    angle = jnp.pi * offset.astype(jnp.float32) / NT
    safe_sin = jnp.where(offset == 0, jnp.float32(1.0), jnp.sin(angle))
    parity = jnp.where(offset % 2 == 0, jnp.float32(1.0), jnp.float32(-1.0))
    deriv = jnp.where(offset == 0, jnp.float32(0.0), 0.5 * parity * jnp.cos(angle) / safe_sin)
    return (deriv + jnp.float32(2.0) / NT).astype(jnp.float32)


def reference(lam_init, rhs, relax, cond, jac, rotor_jac, cols, rotor_shift, owned):
    sectors = SECTORS
    dspec = spectral_matrix()
    row = jnp.arange(NB)
    live = ((row[None, :] >= NB - NR) | (row[None, :] < owned[:, None])).astype(jnp.float32)[None, :, :, None, None]
    lam = lam_init.reshape(NT, sectors, NB, R, BS) * live
    rhs_full = rhs.reshape(NT, sectors, NB, R, BS)
    relax_full = relax.reshape(NT, sectors, NB, 1, BS)
    cond_full = cond.reshape(1, sectors, NB, 1, BS)
    jac_full = jac.reshape(NT, sectors, NB, K, BS, BS)
    rotor_full = rotor_jac.reshape(NT, sectors, NR, BS, BS)
    pattern = cols.reshape(sectors, NB, K)
    moving = rotor_shift.reshape(NT, sectors, NR).astype(jnp.float32)[..., None, None]

    def stator_one(pair):
        padded, blocks = pair
        picked = jax.vmap(lambda hs, cs: hs[cs])(padded, pattern)
        return jnp.einsum('snkri,snkio->snro', picked.astype(jnp.float32), blocks.astype(jnp.float32))

    for sweep in range(SWEEPS):
        lam_b = lam.astype(jnp.bfloat16)
        lam_h = jnp.concatenate([jnp.roll(lam_b, 1, axis=1)[:, :, NB - 1:], lam_b, jnp.roll(lam_b, -1, axis=1)[:, :, :1]], axis=2)
        stator = lax.map(stator_one, (lam_h, jac_full))
        records = jnp.einsum('tsjri,tsjio->tsjro', lam_b[:, :, NB - NR:].astype(jnp.float32), rotor_full.astype(jnp.float32))
        rotor = records * (1.0 - moving) + jnp.roll(records * moving, 1, axis=1)
        rotor_rows = jnp.concatenate([jnp.zeros((NT, sectors, NB - NR, R, BS), jnp.float32), rotor], axis=2)
        spec = jnp.einsum('jt,jsnrc->tsnrc', dspec, lam * cond_full, precision=lax.Precision.HIGHEST)
        resid = rhs_full - (stator + rotor_rows + spec)
        lam = lam + relax_full * resid * live
    return lam.reshape(NT, sectors * NB, R, BS)
```

```python
import jax
import jax.numpy as jnp
from jax import lax
from jax.sharding import PartitionSpec as P

NT = 16
SWEEPS = 2


def padded(cells, sides, width):
    for axis, dim in sides:
        count = lax.axis_size(axis)
        head = lax.slice_in_dim(cells, 0, width, axis=dim)
        tail = lax.slice_in_dim(cells, cells.shape[dim] - width, cells.shape[dim], axis=dim)
        cells = jnp.concatenate(
            [
                lax.ppermute(tail, axis, [(i, (i + 1) % count) for i in range(count)]),
                cells,
                lax.ppermute(head, axis, [((i + 1) % count, i) for i in range(count)]),
            ],
            axis=dim,
        )
    return cells


def shifted(block, axis, distance):
    devices = range(lax.axis_size(axis))
    route = [((i - distance) % len(devices), i) for i in devices]
    return lax.ppermute(block, axis, route)


def spectral_matrix():
    index = jnp.arange(NT)
    offset = index[:, None] - index[None, :]
    angle = jnp.pi * offset.astype(jnp.float32) / NT
    safe_sin = jnp.where(offset == 0, jnp.float32(1.0), jnp.sin(angle))
    parity = jnp.where(offset % 2 == 0, jnp.float32(1.0), jnp.float32(-1.0))
    deriv = jnp.where(offset == 0, jnp.float32(0.0), 0.5 * parity * jnp.cos(angle) / safe_sin)
    return deriv + jnp.float32(2.0) / NT


def column_of(s, dx):
    return (s // 8) * 8 + (((s // 2) % 4 + dx) % 4) * 2 + s % 2


def routed(block, dest):
    return lax.ppermute(block, "inst", [(s, dest(s)) for s in range(lax.axis_size("inst"))])


def instance_mix(weighted, dspec):
    i = lax.axis_index("inst")
    mate = routed(weighted, lambda s: s ^ 1)
    across = routed(weighted, lambda s: s ^ 8)
    diagonal = routed(across, lambda s: s ^ 1)
    members = jnp.stack([i, i ^ 1, i ^ 8, i ^ 9])
    values = (weighted, mate, across, diagonal)

    def partial(target):
        coef = dspec[members, target]
        return sum(coef[k] * values[k] for k in range(4))

    half = weighted.shape[1] // 2
    far = partial(column_of(i, 2))
    ahead = routed(far[:, :half], lambda s: column_of(s, 1))
    behind = routed(far[:, half:], lambda s: column_of(s, 3))
    up = partial(column_of(i, 1))
    up = up.at[:, :half].add(ahead)
    down = partial(column_of(i, 3))
    down = down.at[:, half:].add(behind)
    from_below = routed(up, lambda s: column_of(s, 1))
    from_above = routed(down, lambda s: column_of(s, 3))
    return partial(i) + from_below + from_above


def shards(lam_init, rhs, relax, cond, jac, rotor_jac, cols, rotor_shift, owned):
    local_inst = lam_init.shape[0]
    rows = lam_init.shape[1]
    rotor_rows = rotor_jac.shape[1]
    dspec = spectral_matrix()
    first_inst = lax.axis_index("inst") * local_inst
    row = jnp.arange(rows)
    live = ((row >= rows - rotor_rows) | (row < owned[0])).astype(jnp.float32)[None, :, None, None]
    lam = lam_init * live
    moving = rotor_shift.astype(jnp.float32)[:, :, None, None]
    relax_wide = relax[:, :, None, :]
    cond_wide = cond[None, :, None, :]
    for sweep in range(SWEEPS):
        lam_b = lam.astype(jnp.bfloat16)
        lam_h = padded(lam_b, (("sector", 1),), 1)
        picked = lam_h[:, cols]
        stator = jnp.einsum("tnkri,tnkio->tnro", picked, jac, preferred_element_type=jnp.float32)
        records = jnp.einsum(
            "tjri,tjio->tjro",
            lam_b[:, rows - rotor_rows :],
            rotor_jac,
            preferred_element_type=jnp.float32,
        )
        arrived = shifted((records * moving).astype(jnp.bfloat16), "sector", 1).astype(jnp.float32)
        rotor = records * (1.0 - moving) + arrived
        rotor_full = jnp.concatenate(
            [jnp.zeros((local_inst, rows - rotor_rows) + rotor.shape[2:], jnp.float32), rotor],
            axis=1,
        )
        weighted = lam * cond_wide
        spec = instance_mix(weighted, dspec)
        resid = rhs - (stator + rotor_full + spec)
        lam = lam + relax_wide * resid * live
    return lam


def solution(mesh):
    return jax.shard_map(
        shards,
        mesh=mesh,
        in_specs=(
            P("inst", "sector", None, None),
            P("inst", "sector", None, None),
            P("inst", "sector", None),
            P("sector", None),
            P("inst", "sector", None, None, None),
            P("inst", "sector", None, None),
            P("sector", None),
            P("inst", "sector"),
            P("sector"),
        ),
        out_specs=P("inst", "sector", None, None),
        check_vma=False,
    )
```

```python
import jax
import jax.numpy as jnp
import numpy as np
from jax.experimental import pallas as pl
from jax.experimental.pallas import tpu as pltpu
from jax import lax
from jax.sharding import PartitionSpec as P

NT = 16
SWEEPS = 2


def padded(cells, sides, width):
    for axis, dim in sides:
        count = lax.axis_size(axis)
        head = lax.slice_in_dim(cells, 0, width, axis=dim)
        tail = lax.slice_in_dim(cells, cells.shape[dim] - width, cells.shape[dim], axis=dim)
        cells = jnp.concatenate(
            [
                lax.ppermute(tail, axis, [(i, (i + 1) % count) for i in range(count)]),
                cells,
                lax.ppermute(head, axis, [((i + 1) % count, i) for i in range(count)]),
            ],
            axis=dim,
        )
    return cells


def shifted(block, axis, distance):
    devices = range(lax.axis_size(axis))
    route = [((i - distance) % len(devices), i) for i in devices]
    return lax.ppermute(block, axis, route)


def spectral_matrix():
    index = jnp.arange(NT)
    offset = index[:, None] - index[None, :]
    angle = jnp.pi * offset.astype(jnp.float32) / NT
    safe_sin = jnp.where(offset == 0, jnp.float32(1.0), jnp.sin(angle))
    parity = jnp.where(offset % 2 == 0, jnp.float32(1.0), jnp.float32(-1.0))
    deriv = jnp.where(offset == 0, jnp.float32(0.0), 0.5 * parity * jnp.cos(angle) / safe_sin)
    return deriv + jnp.float32(2.0) / NT


def column_of(s, dx):
    return (s // 8) * 8 + (((s // 2) % 4 + dx) % 4) * 2 + s % 2


def routed(block, dest):
    return lax.ppermute(block, "inst", [(s, dest(s)) for s in range(lax.axis_size("inst"))])


def coefficient_table():
    index = np.arange(NT)
    offset = index[:, None] - index[None, :]
    angle = np.pi * offset / NT
    safe_sin = np.where(offset == 0, 1.0, np.sin(angle))
    parity = np.where(offset % 2 == 0, 1.0, -1.0)
    deriv = np.where(offset == 0, 0.0, 0.5 * parity * np.cos(angle) / safe_sin)
    dspec = deriv + 2.0 / NT
    table = np.zeros((NT, 16), np.float64)
    for s in range(NT):
        members = [s, s ^ 1, s ^ 8, s ^ 9]
        targets = [s, column_of(s, 2), column_of(s, 1), column_of(s, 3)]
        table[s] = [dspec[m, t] for t in targets for m in members]
    return table.astype(np.float32)


def mix_kernel(coef_ref, a_ref, b_ref, c_ref, d_ref, own_ref, far_ref, up_ref, down_ref):
    values = (a_ref[...], b_ref[...], c_ref[...], d_ref[...])
    for slot, out in enumerate((own_ref, far_ref, up_ref, down_ref)):
        acc = coef_ref[slot * 4] * values[0]
        for m in range(1, 4):
            acc = acc + coef_ref[slot * 4 + m] * values[m]
        out[...] = acc


def partial_sums(coef, values):
    rows = values[0].shape[0]
    block = 128
    spec = pl.BlockSpec((block, values[0].shape[1]), lambda r: (r, 0))
    return pl.pallas_call(
        mix_kernel,
        grid=(rows // block,),
        in_specs=[pl.BlockSpec(memory_space=pltpu.SMEM)] + [spec] * 4,
        out_specs=[spec] * 4,
        out_shape=[jax.ShapeDtypeStruct(values[0].shape, jnp.float32)] * 4,
    )(coef, *values)


def instance_mix(weighted):
    i = lax.axis_index("inst")
    shape = weighted.shape
    flat = weighted.reshape(-1, shape[-1])
    across = routed(flat, lambda s: s ^ 8)
    pair = routed(jnp.stack([flat, across]), lambda s: s ^ 1)
    coef = lax.dynamic_slice_in_dim(jnp.asarray(coefficient_table()), i, 1).reshape(-1)
    own, far, up, down = partial_sums(coef, (flat, pair[0], across, pair[1]))
    half = flat.shape[0] // 2
    ahead = routed(far[:half], lambda s: column_of(s, 1))
    behind = routed(far[half:], lambda s: column_of(s, 3))
    up = up + jnp.concatenate([ahead, jnp.zeros_like(behind)])
    down = down + jnp.concatenate([jnp.zeros_like(ahead), behind])
    from_below = routed(up, lambda s: column_of(s, 1))
    from_above = routed(down, lambda s: column_of(s, 3))
    return (own + from_below + from_above).reshape(shape)


def shards(lam_init, rhs, relax, cond, jac, rotor_jac, cols, rotor_shift, owned):
    local_inst = lam_init.shape[0]
    rows = lam_init.shape[1]
    rotor_rows = rotor_jac.shape[1]
    dspec = spectral_matrix()
    first_inst = lax.axis_index("inst") * local_inst
    row = jnp.arange(rows)
    live = ((row >= rows - rotor_rows) | (row < owned[0])).astype(jnp.float32)[None, :, None, None]
    lam = lam_init * live
    moving = rotor_shift.astype(jnp.float32)[:, :, None, None]
    relax_wide = relax[:, :, None, :]
    cond_wide = cond[None, :, None, :]
    for sweep in range(SWEEPS):
        lam_b = lam.astype(jnp.bfloat16)
        lam_h = padded(lam_b, (("sector", 1),), 1)
        picked = lam_h[:, cols]
        stator = jnp.einsum("tnkri,tnkio->tnro", picked, jac, preferred_element_type=jnp.float32)
        records = jnp.einsum(
            "tjri,tjio->tjro",
            lam_b[:, rows - rotor_rows :],
            rotor_jac,
            preferred_element_type=jnp.float32,
        )
        arrived = shifted((records * moving).astype(jnp.bfloat16), "sector", 1).astype(jnp.float32)
        rotor = records * (1.0 - moving) + arrived
        rotor_full = jnp.concatenate(
            [jnp.zeros((local_inst, rows - rotor_rows) + rotor.shape[2:], jnp.float32), rotor],
            axis=1,
        )
        weighted = lam * cond_wide
        spec = instance_mix(weighted)
        resid = rhs - (stator + rotor_full + spec)
        lam = lam + relax_wide * resid * live
    return lam


def solution(mesh):
    return jax.shard_map(
        shards,
        mesh=mesh,
        in_specs=(
            P("inst", "sector", None, None),
            P("inst", "sector", None, None),
            P("inst", "sector", None),
            P("sector", None),
            P("inst", "sector", None, None, None),
            P("inst", "sector", None, None),
            P("sector", None),
            P("inst", "sector"),
            P("sector"),
        ),
        out_specs=P("inst", "sector", None, None),
        check_vma=False,
    )
```

```python
import jax
import jax.numpy as jnp
import numpy as np
from jax.experimental import pallas as pl
from jax.experimental.pallas import tpu as pltpu
from jax import lax
from jax.sharding import PartitionSpec as P

NT = 16
SWEEPS = 2


def padded(cells, sides, width):
    for axis, dim in sides:
        count = lax.axis_size(axis)
        head = lax.slice_in_dim(cells, 0, width, axis=dim)
        tail = lax.slice_in_dim(cells, cells.shape[dim] - width, cells.shape[dim], axis=dim)
        cells = jnp.concatenate(
            [
                lax.ppermute(tail, axis, [(i, (i + 1) % count) for i in range(count)]),
                cells,
                lax.ppermute(head, axis, [((i + 1) % count, i) for i in range(count)]),
            ],
            axis=dim,
        )
    return cells


def shifted(block, axis, distance):
    devices = range(lax.axis_size(axis))
    route = [((i - distance) % len(devices), i) for i in devices]
    return lax.ppermute(block, axis, route)


def spectral_matrix():
    index = jnp.arange(NT)
    offset = index[:, None] - index[None, :]
    angle = jnp.pi * offset.astype(jnp.float32) / NT
    safe_sin = jnp.where(offset == 0, jnp.float32(1.0), jnp.sin(angle))
    parity = jnp.where(offset % 2 == 0, jnp.float32(1.0), jnp.float32(-1.0))
    deriv = jnp.where(offset == 0, jnp.float32(0.0), 0.5 * parity * jnp.cos(angle) / safe_sin)
    return deriv + jnp.float32(2.0) / NT


INST = ("iy", "ix", "ic")


def coefficient_table():
    index = np.arange(NT)
    offset = index[:, None] - index[None, :]
    angle = np.pi * offset / NT
    safe_sin = np.where(offset == 0, 1.0, np.sin(angle))
    parity = np.where(offset % 2 == 0, 1.0, -1.0)
    deriv = np.where(offset == 0, 0.0, 0.5 * parity * np.cos(angle) / safe_sin)
    dspec = deriv + 2.0 / NT
    table = np.zeros((NT, 16), np.float64)
    for s in range(NT):
        y, x, c = s // 8, (s // 2) % 4, s % 2
        members = [(m // 2) * 8 + x * 2 + m % 2 for m in range(4)]
        targets = [y * 8 + column * 2 + c for column in range(4)]
        table[s] = [dspec[m, t] for t in targets for m in members]
    return table.astype(np.float32)


def mix_kernel(coef_ref, v_ref, o_ref):
    values = [v_ref[m] for m in range(4)]
    for slot in range(4):
        acc = coef_ref[slot * 4] * values[0]
        for m in range(1, 4):
            acc = acc + coef_ref[slot * 4 + m] * values[m]
        o_ref[slot] = acc


def partial_sums(coef, stacked):
    _, rows, lanes = stacked.shape
    block = 128
    spec = pl.BlockSpec((4, block, lanes), lambda r: (0, r, 0))
    return pl.pallas_call(
        mix_kernel,
        grid=(rows // block,),
        in_specs=[pl.BlockSpec(memory_space=pltpu.SMEM), spec],
        out_specs=spec,
        out_shape=jax.ShapeDtypeStruct(stacked.shape, jnp.float32),
    )(coef, stacked)


def instance_mix(weighted):
    y, x, c = lax.axis_index("iy"), lax.axis_index("ix"), lax.axis_index("ic")
    i = y * 8 + x * 2 + c
    shape = weighted.shape
    flat = weighted.reshape(-1, shape[-1])
    column = lax.all_gather(flat, ("iy", "ic"), axis=0)
    coef = lax.dynamic_slice_in_dim(jnp.asarray(coefficient_table()), i, 1).reshape(-1)
    partials = partial_sums(coef, column)
    return lax.psum_scatter(partials, "ix", scatter_dimension=0).reshape(shape)


def shards(lam_init, rhs, relax, cond, jac, rotor_jac, cols, rotor_shift, owned):
    local_inst = lam_init.shape[0]
    rows = lam_init.shape[1]
    rotor_rows = rotor_jac.shape[1]
    dspec = spectral_matrix()
    first_inst = 0
    row = jnp.arange(rows)
    live = ((row >= rows - rotor_rows) | (row < owned[0])).astype(jnp.float32)[None, :, None, None]
    lam = lam_init * live
    moving = rotor_shift.astype(jnp.float32)[:, :, None, None]
    relax_wide = relax[:, :, None, :]
    cond_wide = cond[None, :, None, :]
    for sweep in range(SWEEPS):
        lam_b = lam.astype(jnp.bfloat16)
        lam_h = padded(lam_b, (("sector", 1),), 1)
        picked = lam_h[:, cols]
        stator = jnp.einsum("tnkri,tnkio->tnro", picked, jac, preferred_element_type=jnp.float32)
        records = jnp.einsum(
            "tjri,tjio->tjro",
            lam_b[:, rows - rotor_rows :],
            rotor_jac,
            preferred_element_type=jnp.float32,
        )
        arrived = shifted((records * moving).astype(jnp.bfloat16), "sector", 1).astype(jnp.float32)
        rotor = records * (1.0 - moving) + arrived
        rotor_full = jnp.concatenate(
            [jnp.zeros((local_inst, rows - rotor_rows) + rotor.shape[2:], jnp.float32), rotor],
            axis=1,
        )
        weighted = lam * cond_wide
        spec = instance_mix(weighted)
        resid = rhs - (stator + rotor_full + spec)
        lam = lam + relax_wide * resid * live
    return lam


def solution(mesh):
    fine = jax.sharding.Mesh(mesh.devices.reshape(2, 4, 2, -1), INST + ("sector",))
    return jax.shard_map(
        shards,
        mesh=fine,
        in_specs=(
            P(INST, "sector", None, None),
            P(INST, "sector", None, None),
            P(INST, "sector", None),
            P("sector", None),
            P(INST, "sector", None, None, None),
            P(INST, "sector", None, None),
            P("sector", None),
            P(INST, "sector"),
            P("sector"),
        ),
        out_specs=P(INST, "sector", None, None),
        check_vma=False,
    )
```

```python
import jax
import jax.numpy as jnp
import numpy as np
from jax.experimental import pallas as pl
from jax.experimental.pallas import tpu as pltpu
from jax import lax
from jax.sharding import PartitionSpec as P

NT = 16
SWEEPS = 2


def padded(cells, sides, width):
    for axis, dim in sides:
        count = lax.axis_size(axis)
        head = lax.slice_in_dim(cells, 0, width, axis=dim)
        tail = lax.slice_in_dim(cells, cells.shape[dim] - width, cells.shape[dim], axis=dim)
        cells = jnp.concatenate(
            [
                lax.ppermute(tail, axis, [(i, (i + 1) % count) for i in range(count)]),
                cells,
                lax.ppermute(head, axis, [((i + 1) % count, i) for i in range(count)]),
            ],
            axis=dim,
        )
    return cells


def shifted(block, axis, distance):
    devices = range(lax.axis_size(axis))
    route = [((i - distance) % len(devices), i) for i in devices]
    return lax.ppermute(block, axis, route)


def spectral_matrix():
    index = jnp.arange(NT)
    offset = index[:, None] - index[None, :]
    angle = jnp.pi * offset.astype(jnp.float32) / NT
    safe_sin = jnp.where(offset == 0, jnp.float32(1.0), jnp.sin(angle))
    parity = jnp.where(offset % 2 == 0, jnp.float32(1.0), jnp.float32(-1.0))
    deriv = jnp.where(offset == 0, jnp.float32(0.0), 0.5 * parity * jnp.cos(angle) / safe_sin)
    return deriv + jnp.float32(2.0) / NT


def column_of(s, dx):
    return (s // 8) * 8 + (((s // 2) % 4 + dx) % 4) * 2 + s % 2


def routed(block, dest):
    return lax.ppermute(block, "inst", [(s, dest(s)) for s in range(lax.axis_size("inst"))])


def coefficient_table():
    index = np.arange(NT)
    offset = index[:, None] - index[None, :]
    angle = np.pi * offset / NT
    safe_sin = np.where(offset == 0, 1.0, np.sin(angle))
    parity = np.where(offset % 2 == 0, 1.0, -1.0)
    deriv = np.where(offset == 0, 0.0, 0.5 * parity * np.cos(angle) / safe_sin)
    dspec = deriv + 2.0 / NT
    table = np.zeros((NT, 16), np.float64)
    for s in range(NT):
        members = [s, s ^ 1, s ^ 8, s ^ 9]
        targets = [s, column_of(s, 2), column_of(s, 1), column_of(s, 3)]
        table[s] = [dspec[m, t] for t in targets for m in members]
    return table.astype(np.float32)


def mix_kernel(coef_ref, a_ref, b_ref, c_ref, d_ref, own_ref, far_ref, up_ref, down_ref):
    values = (a_ref[...], b_ref[...], c_ref[...], d_ref[...])
    for slot, out in enumerate((own_ref, far_ref, up_ref, down_ref)):
        acc = coef_ref[slot * 4] * values[0]
        for m in range(1, 4):
            acc = acc + coef_ref[slot * 4 + m] * values[m]
        out[...] = acc


def partial_sums(coef, values):
    rows = values[0].shape[0]
    block = 128
    spec = pl.BlockSpec((block, values[0].shape[1]), lambda r: (r, 0))
    return pl.pallas_call(
        mix_kernel,
        grid=(rows // block,),
        in_specs=[pl.BlockSpec(memory_space=pltpu.SMEM)] + [spec] * 4,
        out_specs=[spec] * 4,
        out_shape=[jax.ShapeDtypeStruct(values[0].shape, jnp.float32)] * 4,
    )(coef, *values)


def instance_mix(weighted):
    i = lax.axis_index("inst")
    shape = weighted.shape
    flat = weighted.reshape(-1, shape[-1])
    across = routed(flat, lambda s: s ^ 8)
    pair = routed(jnp.stack([flat, across]), lambda s: s ^ 1)
    coef = lax.dynamic_slice_in_dim(jnp.asarray(coefficient_table()), i, 1).reshape(-1)
    own, far, up, down = partial_sums(coef, (flat, pair[0], across, pair[1]))
    from_far = routed(far, lambda s: column_of(s, 2))
    from_below = routed(up, lambda s: column_of(s, 1))
    from_above = routed(down, lambda s: column_of(s, 3))
    return (own + from_far + from_below + from_above).reshape(shape)


def shards(lam_init, rhs, relax, cond, jac, rotor_jac, cols, rotor_shift, owned):
    local_inst = lam_init.shape[0]
    rows = lam_init.shape[1]
    rotor_rows = rotor_jac.shape[1]
    dspec = spectral_matrix()
    first_inst = lax.axis_index("inst") * local_inst
    row = jnp.arange(rows)
    live = ((row >= rows - rotor_rows) | (row < owned[0])).astype(jnp.float32)[None, :, None, None]
    lam = lam_init * live
    moving = rotor_shift.astype(jnp.float32)[:, :, None, None]
    relax_wide = relax[:, :, None, :]
    cond_wide = cond[None, :, None, :]
    for sweep in range(SWEEPS):
        lam_b = lam.astype(jnp.bfloat16)
        records = jnp.einsum(
            "tjri,tjio->tjro",
            lam_b[:, rows - rotor_rows :],
            rotor_jac,
            preferred_element_type=jnp.float32,
        )
        onward = jnp.concatenate([lam_b[:, rows - 1 :], (records * moving).astype(jnp.bfloat16)], axis=1)
        onward = shifted(onward, "sector", 1)
        head = shifted(lam_b[:, :1], "sector", -1)
        lam_h = jnp.concatenate([onward[:, :1], lam_b, head], axis=1)
        picked = lam_h[:, cols]
        stator = jnp.einsum("tnkri,tnkio->tnro", picked, jac, preferred_element_type=jnp.float32)
        arrived = onward[:, 1:].astype(jnp.float32)
        rotor = records * (1.0 - moving) + arrived
        rotor_full = jnp.concatenate(
            [jnp.zeros((local_inst, rows - rotor_rows) + rotor.shape[2:], jnp.float32), rotor],
            axis=1,
        )
        weighted = lam * cond_wide
        spec = instance_mix(weighted)
        resid = rhs - (stator + rotor_full + spec)
        lam = lam + relax_wide * resid * live
    return lam


def solution(mesh):
    return jax.shard_map(
        shards,
        mesh=mesh,
        in_specs=(
            P("inst", "sector", None, None),
            P("inst", "sector", None, None),
            P("inst", "sector", None),
            P("sector", None),
            P("inst", "sector", None, None, None),
            P("inst", "sector", None, None),
            P("sector", None),
            P("inst", "sector"),
            P("sector"),
        ),
        out_specs=P("inst", "sector", None, None),
        check_vma=False,
    )
```

```python
import jax
import jax.numpy as jnp
import numpy as np
from jax.experimental import pallas as pl
from jax.experimental.pallas import tpu as pltpu
from jax import lax
from jax.sharding import PartitionSpec as P

NT = 16
SWEEPS = 2


def padded(cells, sides, width):
    for axis, dim in sides:
        count = lax.axis_size(axis)
        head = lax.slice_in_dim(cells, 0, width, axis=dim)
        tail = lax.slice_in_dim(cells, cells.shape[dim] - width, cells.shape[dim], axis=dim)
        cells = jnp.concatenate(
            [
                lax.ppermute(tail, axis, [(i, (i + 1) % count) for i in range(count)]),
                cells,
                lax.ppermute(head, axis, [((i + 1) % count, i) for i in range(count)]),
            ],
            axis=dim,
        )
    return cells


def shifted(block, axis, distance):
    devices = range(lax.axis_size(axis))
    route = [((i - distance) % len(devices), i) for i in devices]
    return lax.ppermute(block, axis, route)


def spectral_matrix():
    index = jnp.arange(NT)
    offset = index[:, None] - index[None, :]
    angle = jnp.pi * offset.astype(jnp.float32) / NT
    safe_sin = jnp.where(offset == 0, jnp.float32(1.0), jnp.sin(angle))
    parity = jnp.where(offset % 2 == 0, jnp.float32(1.0), jnp.float32(-1.0))
    deriv = jnp.where(offset == 0, jnp.float32(0.0), 0.5 * parity * jnp.cos(angle) / safe_sin)
    return deriv + jnp.float32(2.0) / NT


INST = ("iy", "ix", "ic")


def routed(block, dest):
    return lax.ppermute(block, INST, [(s, dest(s)) for s in range(NT)])


def coefficient_table():
    index = np.arange(NT)
    offset = index[:, None] - index[None, :]
    angle = np.pi * offset / NT
    safe_sin = np.where(offset == 0, 1.0, np.sin(angle))
    parity = np.where(offset % 2 == 0, 1.0, -1.0)
    deriv = np.where(offset == 0, 0.0, 0.5 * parity * np.cos(angle) / safe_sin)
    dspec = deriv + 2.0 / NT
    table = np.zeros((NT, 16), np.float64)
    for s in range(NT):
        y, x, c = s // 8, (s // 2) % 4, s % 2
        members = [s, s ^ 1, s ^ 8, s ^ 9]
        targets = [y * 8 + column * 2 + c for column in range(4)]
        table[s] = [dspec[m, t] for t in targets for m in members]
    return table.astype(np.float32)


def mix_kernel(coef_ref, own_ref, across_ref, pair_ref, o_ref):
    values = (own_ref[...], pair_ref[0], across_ref[...], pair_ref[1])
    for slot in range(4):
        acc = coef_ref[slot * 4] * values[0]
        for m in range(1, 4):
            acc = acc + coef_ref[slot * 4 + m] * values[m]
        o_ref[slot] = acc


def partial_sums(coef, own, across, pair):
    rows, lanes = own.shape
    block = 256
    flat = pl.BlockSpec((block, lanes), lambda r: (r, 0))
    stacked = pl.BlockSpec((2, block, lanes), lambda r: (0, r, 0))
    return pl.pallas_call(
        mix_kernel,
        grid=(rows // block,),
        in_specs=[pl.BlockSpec(memory_space=pltpu.SMEM), flat, flat, stacked],
        out_specs=pl.BlockSpec((4, block, lanes), lambda r: (0, r, 0)),
        out_shape=jax.ShapeDtypeStruct((4, rows, lanes), jnp.float32),
    )(coef, own, across, pair)


def instance_mix(weighted):
    i = lax.axis_index("iy") * 8 + lax.axis_index("ix") * 2 + lax.axis_index("ic")
    shape = weighted.shape
    flat = weighted.reshape(-1, shape[-1])
    across = routed(flat, lambda s: s ^ 8)
    pair = routed(jnp.stack([flat, across]), lambda s: s ^ 1)
    coef = lax.dynamic_slice_in_dim(jnp.asarray(coefficient_table()), i, 1).reshape(-1)
    partials = partial_sums(coef, flat, across, pair)
    gathered = lax.all_to_all(partials, "ix", 0, 0)
    return gathered.sum(axis=0).reshape(shape)


def shards(lam_init, rhs, relax, cond, jac, rotor_jac, cols, rotor_shift, owned):
    local_inst = lam_init.shape[0]
    rows = lam_init.shape[1]
    rotor_rows = rotor_jac.shape[1]
    dspec = spectral_matrix()
    row = jnp.arange(rows)
    live = ((row >= rows - rotor_rows) | (row < owned[0])).astype(jnp.float32)[None, :, None, None]
    lam = lam_init * live
    moving = rotor_shift.astype(jnp.float32)[:, :, None, None]
    relax_wide = relax[:, :, None, :]
    cond_wide = cond[None, :, None, :]
    for sweep in range(SWEEPS):
        lam_b = lam.astype(jnp.bfloat16)
        records = jnp.einsum(
            "tjri,tjio->tjro",
            lam_b[:, rows - rotor_rows :],
            rotor_jac,
            preferred_element_type=jnp.float32,
        )
        onward = jnp.concatenate([lam_b[:, rows - 1 :], (records * moving).astype(jnp.bfloat16)], axis=1)
        onward = shifted(onward, "sector", 1)
        head = shifted(lam_b[:, :1], "sector", -1)
        lam_h = jnp.concatenate([onward[:, :1], lam_b, head], axis=1)
        picked = lam_h[:, cols]
        stator = jnp.einsum("tnkri,tnkio->tnro", picked, jac, preferred_element_type=jnp.float32)
        arrived = onward[:, 1:].astype(jnp.float32)
        rotor = records * (1.0 - moving) + arrived
        rotor_full = jnp.concatenate(
            [jnp.zeros((local_inst, rows - rotor_rows) + rotor.shape[2:], jnp.float32), rotor],
            axis=1,
        )
        weighted = lam * cond_wide
        spec = instance_mix(weighted)
        resid = rhs - (stator + rotor_full + spec)
        lam = lam + relax_wide * resid * live
    return lam


def solution(mesh):
    fine = jax.sharding.Mesh(mesh.devices.reshape(2, 4, 2, -1), INST + ("sector",))
    return jax.shard_map(
        shards,
        mesh=fine,
        in_specs=(
            P(INST, "sector", None, None),
            P(INST, "sector", None, None),
            P(INST, "sector", None),
            P("sector", None),
            P(INST, "sector", None, None, None),
            P(INST, "sector", None, None),
            P("sector", None),
            P(INST, "sector"),
            P("sector"),
        ),
        out_specs=P(INST, "sector", None, None),
        check_vma=False,
    )
```

```python
import jax
import jax.numpy as jnp
import numpy as np
from jax.experimental import pallas as pl
from jax.experimental.pallas import tpu as pltpu
from jax import lax
from jax.sharding import PartitionSpec as P

NT = 16
SWEEPS = 2


def padded(cells, sides, width):
    for axis, dim in sides:
        count = lax.axis_size(axis)
        head = lax.slice_in_dim(cells, 0, width, axis=dim)
        tail = lax.slice_in_dim(cells, cells.shape[dim] - width, cells.shape[dim], axis=dim)
        cells = jnp.concatenate(
            [
                lax.ppermute(tail, axis, [(i, (i + 1) % count) for i in range(count)]),
                cells,
                lax.ppermute(head, axis, [((i + 1) % count, i) for i in range(count)]),
            ],
            axis=dim,
        )
    return cells


def shifted(block, axis, distance):
    devices = range(lax.axis_size(axis))
    route = [((i - distance) % len(devices), i) for i in devices]
    return lax.ppermute(block, axis, route)


def spectral_matrix():
    index = jnp.arange(NT)
    offset = index[:, None] - index[None, :]
    angle = jnp.pi * offset.astype(jnp.float32) / NT
    safe_sin = jnp.where(offset == 0, jnp.float32(1.0), jnp.sin(angle))
    parity = jnp.where(offset % 2 == 0, jnp.float32(1.0), jnp.float32(-1.0))
    deriv = jnp.where(offset == 0, jnp.float32(0.0), 0.5 * parity * jnp.cos(angle) / safe_sin)
    return deriv + jnp.float32(2.0) / NT


INST = ("iy", "ix", "ic")


def routed(block, dest):
    return lax.ppermute(block, INST, [(s, dest(s)) for s in range(NT)])


def coefficient_table():
    index = np.arange(NT)
    offset = index[:, None] - index[None, :]
    angle = np.pi * offset / NT
    safe_sin = np.where(offset == 0, 1.0, np.sin(angle))
    parity = np.where(offset % 2 == 0, 1.0, -1.0)
    deriv = np.where(offset == 0, 0.0, 0.5 * parity * np.cos(angle) / safe_sin)
    dspec = deriv + 2.0 / NT
    table = np.zeros((NT, 16), np.float64)
    for s in range(NT):
        y, x, c = s // 8, (s // 2) % 4, s % 2
        members = [s, s ^ 1, s ^ 8, s ^ 9]
        targets = [y * 8 + column * 2 + c for column in range(4)]
        table[s] = [dspec[m, t] for t in targets for m in members]
    return table.astype(np.float32)


def mix_kernel(index_ref, coef_ref, own_ref, across_ref, pair_ref, o_ref):
    me = index_ref[0]
    values = (own_ref[...], pair_ref[0], across_ref[...], pair_ref[1])
    for slot in range(4):
        acc = coef_ref[me, slot * 4] * values[0]
        for m in range(1, 4):
            acc = acc + coef_ref[me, slot * 4 + m] * values[m]
        o_ref[slot] = acc


def partial_sums(index, own, across, pair):
    rows, lanes = own.shape
    block = 256
    flat = pl.BlockSpec((block, lanes), lambda r, index: (r, 0))
    stacked = pl.BlockSpec((2, block, lanes), lambda r, index: (0, r, 0))
    return pl.pallas_call(
        mix_kernel,
        grid_spec=pltpu.PrefetchScalarGridSpec(
            num_scalar_prefetch=1,
            grid=(rows // block,),
            in_specs=[pl.BlockSpec(memory_space=pltpu.SMEM), flat, flat, stacked],
            out_specs=pl.BlockSpec((4, block, lanes), lambda r, index: (0, r, 0)),
        ),
        out_shape=jax.ShapeDtypeStruct((4, rows, lanes), jnp.float32),
    )(index, jnp.asarray(coefficient_table()), own, across, pair)


def instance_mix(weighted):
    i = lax.axis_index("iy") * 8 + lax.axis_index("ix") * 2 + lax.axis_index("ic")
    shape = weighted.shape
    flat = weighted.reshape(-1, shape[-1])
    across = routed(flat, lambda s: s ^ 8)
    pair = routed(jnp.stack([flat, across]), lambda s: s ^ 1)
    partials = partial_sums(jnp.reshape(i, (1,)).astype(jnp.int32), flat, across, pair)
    gathered = lax.all_to_all(partials, "ix", 0, 0)
    return partials, [gathered[k].reshape(shape) for k in range(gathered.shape[0])]


def shards(lam_init, rhs, relax, cond, jac, rotor_jac, cols, rotor_shift, owned):
    local_inst = lam_init.shape[0]
    rows = lam_init.shape[1]
    rotor_rows = rotor_jac.shape[1]
    dspec = spectral_matrix()
    row = jnp.arange(rows)
    live = ((row >= rows - rotor_rows) | (row < owned[0])).astype(jnp.float32)[None, :, None, None]
    lam = lam_init * live
    moving = rotor_shift.astype(jnp.float32)[:, :, None, None]
    relax_wide = relax[:, :, None, :]
    cond_wide = cond[None, :, None, :]
    for sweep in range(SWEEPS):
        lam_b = lam.astype(jnp.bfloat16)
        weighted = lam * cond_wide
        partials, pieces = instance_mix(weighted)
        records = jnp.einsum(
            "tjri,tjio->tjro",
            lam_b[:, rows - rotor_rows :],
            rotor_jac,
            preferred_element_type=jnp.float32,
        )
        onward = jnp.concatenate([lam_b[:, rows - 1 :], (records * moving).astype(jnp.bfloat16)], axis=1)
        onward, lam_b, _ = lax.optimization_barrier((onward, lam_b, partials))
        onward = shifted(onward, "sector", 1)
        head = shifted(lam_b[:, :1], "sector", -1)
        lam_h = jnp.concatenate([onward[:, :1], lam_b, head], axis=1)
        picked = lam_h[:, cols]
        stator = jnp.einsum("tnkri,tnkio->tnro", picked, jac, preferred_element_type=jnp.float32)
        arrived = onward[:, 1:].astype(jnp.float32)
        rotor = records * (1.0 - moving) + arrived
        rotor_full = jnp.concatenate(
            [jnp.zeros((local_inst, rows - rotor_rows) + rotor.shape[2:], jnp.float32), rotor],
            axis=1,
        )
        spec = pieces[0] + pieces[1] + pieces[2] + pieces[3]
        resid = rhs - (stator + rotor_full + spec)
        lam = lam + relax_wide * resid * live
    return lam


def solution(mesh):
    fine = jax.sharding.Mesh(mesh.devices.reshape(2, 4, 2, -1), INST + ("sector",))
    return jax.shard_map(
        shards,
        mesh=fine,
        in_specs=(
            P(INST, "sector", None, None),
            P(INST, "sector", None, None),
            P(INST, "sector", None),
            P("sector", None),
            P(INST, "sector", None, None, None),
            P(INST, "sector", None, None),
            P("sector", None),
            P(INST, "sector"),
            P("sector"),
        ),
        out_specs=P(INST, "sector", None, None),
        check_vma=False,
    )
```

```python
import jax
import jax.numpy as jnp
import numpy as np
from jax.experimental import pallas as pl
from jax.experimental.pallas import tpu as pltpu
from jax import lax
from jax.sharding import PartitionSpec as P

NT = 16
SWEEPS = 2


def padded(cells, sides, width):
    for axis, dim in sides:
        count = lax.axis_size(axis)
        head = lax.slice_in_dim(cells, 0, width, axis=dim)
        tail = lax.slice_in_dim(cells, cells.shape[dim] - width, cells.shape[dim], axis=dim)
        cells = jnp.concatenate(
            [
                lax.ppermute(tail, axis, [(i, (i + 1) % count) for i in range(count)]),
                cells,
                lax.ppermute(head, axis, [((i + 1) % count, i) for i in range(count)]),
            ],
            axis=dim,
        )
    return cells


def shifted(block, axis, distance):
    devices = range(lax.axis_size(axis))
    route = [((i - distance) % len(devices), i) for i in devices]
    return lax.ppermute(block, axis, route)


def spectral_matrix():
    index = jnp.arange(NT)
    offset = index[:, None] - index[None, :]
    angle = jnp.pi * offset.astype(jnp.float32) / NT
    safe_sin = jnp.where(offset == 0, jnp.float32(1.0), jnp.sin(angle))
    parity = jnp.where(offset % 2 == 0, jnp.float32(1.0), jnp.float32(-1.0))
    deriv = jnp.where(offset == 0, jnp.float32(0.0), 0.5 * parity * jnp.cos(angle) / safe_sin)
    return deriv + jnp.float32(2.0) / NT


INST = ("iy", "ix", "ic")


def routed(block, dest):
    return lax.ppermute(block, INST, [(s, dest(s)) for s in range(NT)])


def spectral_numpy():
    index = np.arange(NT)
    offset = index[:, None] - index[None, :]
    angle = np.pi * offset / NT
    safe_sin = np.where(offset == 0, 1.0, np.sin(angle))
    parity = np.where(offset % 2 == 0, 1.0, -1.0)
    deriv = np.where(offset == 0, 0.0, 0.5 * parity * np.cos(angle) / safe_sin)
    return deriv + 2.0 / NT


def members_of(s):
    return [s, s ^ 1, s ^ 8, s ^ 9]


def targets_of(s):
    return [(s // 8) * 8 + column * 2 + s % 2 for column in range(4)]


def coefficient_table():
    dspec = spectral_numpy()
    table = np.zeros((NT, 16), np.float64)
    for s in range(NT):
        table[s] = [dspec[m, t] for t in targets_of(s) for m in members_of(s)]
    return table.astype(np.float32)


def second_table():
    dspec = spectral_numpy()
    table = np.zeros((NT, 4, 4, 16), np.float64)
    for s in range(NT):
        slots = [u for t in targets_of(s) for u in members_of(t)]
        for mv, v in enumerate(members_of(s)):
            for k, t in enumerate(targets_of(s)):
                table[s, mv, k] = [dspec[v, u] * dspec[u, t] for u in slots]
    return table.astype(np.float32)


def column_kernel(index_ref, coef_ref, own_ref, across_ref, pair_ref, o_ref):
    me = index_ref[0]
    span = own_ref.shape[0]
    extra = (o_ref.shape[1] - span) // 3
    rows = span - extra
    values = (own_ref[:rows], pair_ref[0, :rows], across_ref[:rows], pair_ref[1, :rows])
    for slot in range(4):
        acc = coef_ref[me, slot * 4] * values[0]
        for m in range(1, 4):
            acc = acc + coef_ref[me, slot * 4 + m] * values[m]
        o_ref[slot, :rows] = acc
        if extra:
            o_ref[slot, rows : rows + extra] = own_ref[rows:]
            o_ref[slot, rows + extra : rows + 2 * extra] = pair_ref[0, rows:]
            o_ref[slot, rows + 2 * extra : rows + 3 * extra] = across_ref[rows:]
            o_ref[slot, rows + 3 * extra : rows + 4 * extra] = pair_ref[1, rows:]


def column_partials(index, own, across, pair, rows):
    span, lanes = own.shape
    extra = span - rows
    return pl.pallas_call(
        column_kernel,
        grid_spec=pltpu.PrefetchScalarGridSpec(
            num_scalar_prefetch=1,
            grid=(1,),
            in_specs=[
                pl.BlockSpec(memory_space=pltpu.SMEM),
                pl.BlockSpec((span, lanes), lambda r, index: (0, 0)),
                pl.BlockSpec((span, lanes), lambda r, index: (0, 0)),
                pl.BlockSpec((2, span, lanes), lambda r, index: (0, 0, 0)),
            ],
            out_specs=pl.BlockSpec((4, rows + 4 * extra, lanes), lambda r, index: (0, 0, 0)),
        ),
        out_shape=jax.ShapeDtypeStruct((4, rows + 4 * extra, lanes), jnp.float32),
    )(index, jnp.asarray(coefficient_table()), own, across, pair)


def column_stage(flat):
    across = routed(flat, lambda s: s ^ 8)
    pair = routed(jnp.stack([flat, across]), lambda s: s ^ 1)
    return across, pair


def shards(lam_init, rhs, relax, cond, jac, rotor_jac, cols, rotor_shift, owned):
    local_inst, rows, reps, lanes = lam_init.shape
    rotor_rows = rotor_jac.shape[1]
    i = lax.axis_index("iy") * 8 + lax.axis_index("ix") * 2 + lax.axis_index("ic")
    index = jnp.reshape(i, (1,)).astype(jnp.int32)
    row = jnp.arange(rows)
    live_rows = ((row >= rows - rotor_rows) | (row < owned[0])).astype(jnp.float32)
    live = live_rows[None, :, None, None]
    moving = rotor_shift.astype(jnp.float32)[:, :, None, None]
    relax_wide = relax[:, :, None, :]
    cond_wide = cond[None, :, None, :]
    body = rows * reps

    def local_operator(lam):
        lam_b = lam.astype(jnp.bfloat16)
        records = jnp.einsum(
            "tjri,tjio->tjro",
            lam_b[:, rows - rotor_rows :],
            rotor_jac,
            preferred_element_type=jnp.float32,
        )
        onward = jnp.concatenate([lam_b[:, rows - 1 :], (records * moving).astype(jnp.bfloat16)], axis=1)
        onward = shifted(onward, "sector", 1)
        head = shifted(lam_b[:, :1], "sector", -1)
        lam_h = jnp.concatenate([onward[:, :1], lam_b, head], axis=1)
        picked = lam_h[:, cols]
        stator = jnp.einsum("tnkri,tnkio->tnro", picked, jac, preferred_element_type=jnp.float32)
        arrived = onward[:, 1:].astype(jnp.float32)
        rotor = records * (1.0 - moving) + arrived
        rotor_full = jnp.concatenate(
            [jnp.zeros((local_inst, rows - rotor_rows) + rotor.shape[2:], jnp.float32), rotor],
            axis=1,
        )
        return stator + rotor_full

    lam0 = lam_init * live
    w0 = (lam0 * cond_wide).reshape(body, lanes)
    carried = jnp.concatenate([w0, relax.reshape(rows, lanes)])
    across0, pair0 = column_stage(carried)
    first = column_partials(index, carried, across0, pair0, body)
    got0 = lax.all_to_all(first, "ix", 0, 0)

    local0 = local_operator(lax.optimization_barrier((lam0, first))[0])
    base = lam0 + relax_wide * (rhs - local0) * live
    wb = (base * cond_wide).reshape(body, lanes)
    across1, pair1 = column_stage(wb)
    got0, across1, pair1 = lax.optimization_barrier((got0, across1, pair1))

    spec0 = (got0[0, :body] + got0[1, :body] + got0[2, :body] + got0[3, :body]).reshape(lam0.shape)
    lam1 = base - relax_wide * spec0 * live

    relax_all = got0[:, body:].reshape(16, rows, lanes)
    pairs = lax.dynamic_slice_in_dim(jnp.asarray(second_table()), i, 1)[0]
    kernel2 = jnp.einsum("vks,snb->vknb", pairs, relax_all, precision=lax.Precision.HIGHEST)
    kernel2 = kernel2 * live_rows[None, None, :, None] * cond[None, None]
    w0col = jnp.stack([w0, pair0[0, :body], across0[:body], pair0[1, :body]]).reshape(4, rows, reps, lanes)
    wbcol = jnp.stack([wb, pair1[0], across1, pair1[1]]).reshape(4, rows, reps, lanes)
    coef = lax.dynamic_slice_in_dim(jnp.asarray(coefficient_table()), i, 1).reshape(4, 4)
    second = jnp.einsum("km,mnrb->knrb", coef, wbcol, precision=lax.Precision.HIGHEST) - jnp.einsum(
        "mknb,mnrb->knrb", kernel2, w0col, precision=lax.Precision.HIGHEST
    )
    got1 = lax.all_to_all(second.reshape(4, body, lanes), "ix", 0, 0)
    spec1 = (got1[0] + got1[1] + got1[2] + got1[3]).reshape(lam0.shape)

    local1 = local_operator(lam1)
    return lam1 + relax_wide * (rhs - (local1 + spec1)) * live


def solution(mesh):
    fine = jax.sharding.Mesh(mesh.devices.reshape(2, 4, 2, -1), INST + ("sector",))
    return jax.shard_map(
        shards,
        mesh=fine,
        in_specs=(
            P(INST, "sector", None, None),
            P(INST, "sector", None, None),
            P(INST, "sector", None),
            P("sector", None),
            P(INST, "sector", None, None, None),
            P(INST, "sector", None, None),
            P("sector", None),
            P(INST, "sector"),
            P("sector"),
        ),
        out_specs=P(INST, "sector", None, None),
        check_vma=False,
    )
```

```python
import jax
import jax.numpy as jnp
import numpy as np
from jax.experimental import pallas as pl
from jax.experimental.pallas import tpu as pltpu
from jax import lax
from jax.sharding import PartitionSpec as P

NT = 16
SWEEPS = 2


def padded(cells, sides, width):
    for axis, dim in sides:
        count = lax.axis_size(axis)
        head = lax.slice_in_dim(cells, 0, width, axis=dim)
        tail = lax.slice_in_dim(cells, cells.shape[dim] - width, cells.shape[dim], axis=dim)
        cells = jnp.concatenate(
            [
                lax.ppermute(tail, axis, [(i, (i + 1) % count) for i in range(count)]),
                cells,
                lax.ppermute(head, axis, [((i + 1) % count, i) for i in range(count)]),
            ],
            axis=dim,
        )
    return cells


def shifted(block, axis, distance):
    devices = range(lax.axis_size(axis))
    route = [((i - distance) % len(devices), i) for i in devices]
    return lax.ppermute(block, axis, route)


def spectral_matrix():
    index = jnp.arange(NT)
    offset = index[:, None] - index[None, :]
    angle = jnp.pi * offset.astype(jnp.float32) / NT
    safe_sin = jnp.where(offset == 0, jnp.float32(1.0), jnp.sin(angle))
    parity = jnp.where(offset % 2 == 0, jnp.float32(1.0), jnp.float32(-1.0))
    deriv = jnp.where(offset == 0, jnp.float32(0.0), 0.5 * parity * jnp.cos(angle) / safe_sin)
    return deriv + jnp.float32(2.0) / NT


INST = ("iy", "ix", "ic")


def routed(block, dest):
    return lax.ppermute(block, INST, [(s, dest(s)) for s in range(NT)])


def coefficient_table():
    index = np.arange(NT)
    offset = index[:, None] - index[None, :]
    angle = np.pi * offset / NT
    safe_sin = np.where(offset == 0, 1.0, np.sin(angle))
    parity = np.where(offset % 2 == 0, 1.0, -1.0)
    deriv = np.where(offset == 0, 0.0, 0.5 * parity * np.cos(angle) / safe_sin)
    dspec = deriv + 2.0 / NT
    table = np.zeros((NT, 16), np.float64)
    for s in range(NT):
        y, x, c = s // 8, (s // 2) % 4, s % 2
        members = [s, s ^ 1, s ^ 8, s ^ 9]
        targets = [y * 8 + column * 2 + c for column in range(4)]
        table[s] = [dspec[m, t] for t in targets for m in members]
    return table.astype(np.float32)


def mix_kernel(index_ref, coef_ref, own_ref, mate_ref, across_ref, diagonal_ref, o_ref):
    me = index_ref[0]
    values = (own_ref[...], mate_ref[...], across_ref[...], diagonal_ref[...])
    for slot in range(4):
        acc = coef_ref[me, slot * 4] * values[0]
        for m in range(1, 4):
            acc = acc + coef_ref[me, slot * 4 + m] * values[m]
        o_ref[slot] = acc


def partial_sums(index, own, mate, across, diagonal):
    rows, lanes = own.shape
    block = 256
    flat = pl.BlockSpec((block, lanes), lambda r, index: (r, 0))
    return pl.pallas_call(
        mix_kernel,
        grid_spec=pltpu.PrefetchScalarGridSpec(
            num_scalar_prefetch=1,
            grid=(rows // block,),
            in_specs=[pl.BlockSpec(memory_space=pltpu.SMEM), flat, flat, flat, flat],
            out_specs=pl.BlockSpec((4, block, lanes), lambda r, index: (0, r, 0)),
        ),
        out_shape=jax.ShapeDtypeStruct((4, rows, lanes), jnp.float32),
    )(index, jnp.asarray(coefficient_table()), own, mate, across, diagonal)


def update_kernel(got_ref, base_ref, scale_ref, cond_ref, lam_ref, weighted_ref):
    spec = (got_ref[0] + got_ref[1]) + (got_ref[2] + got_ref[3])
    lam = base_ref[...] - scale_ref[...] * spec
    lam_ref[...] = lam
    weighted_ref[...] = lam * cond_ref[...]


def updated(got, base, scale, condb):
    rows, lanes = base.shape
    block = 256
    flat = pl.BlockSpec((block, lanes), lambda r: (r, 0))
    return pl.pallas_call(
        update_kernel,
        grid=(rows // block,),
        in_specs=[pl.BlockSpec((4, block, lanes), lambda r: (0, r, 0)), flat, flat, flat],
        out_specs=[flat, flat],
        out_shape=[jax.ShapeDtypeStruct(base.shape, jnp.float32)] * 2,
    )(got, base, scale, condb)


def instance_mix(flat):
    i = lax.axis_index("iy") * 8 + lax.axis_index("ix") * 2 + lax.axis_index("ic")
    mate = routed(flat, lambda s: s ^ 1)
    across = routed(flat, lambda s: s ^ 8)
    diagonal = routed(across, lambda s: s ^ 1)
    partials = partial_sums(jnp.reshape(i, (1,)).astype(jnp.int32), flat, mate, across, diagonal)
    return partials, lax.all_to_all(partials, "ix", 0, 0)


def shards(lam_init, rhs, relax, cond, jac, rotor_jac, cols, rotor_shift, owned):
    local_inst = lam_init.shape[0]
    rows = lam_init.shape[1]
    rotor_rows = rotor_jac.shape[1]
    shape = lam_init.shape
    lanes = shape[-1]
    row = jnp.arange(rows)
    live = ((row >= rows - rotor_rows) | (row < owned[0])).astype(jnp.float32)[None, :, None, None]
    lam = lam_init * live
    moving = rotor_shift.astype(jnp.float32)[:, :, None, None]
    relax_wide = relax[:, :, None, :]
    cond_wide = cond[None, :, None, :]
    scale = jnp.broadcast_to(relax_wide * live, shape).reshape(-1, lanes)
    condb = jnp.broadcast_to(cond_wide, shape).reshape(-1, lanes)
    weighted = (lam * cond_wide).reshape(-1, lanes)
    for sweep in range(SWEEPS):
        lam_b = lam.astype(jnp.bfloat16)
        partials, got = instance_mix(weighted)
        records = jnp.einsum(
            "tjri,tjio->tjro",
            lam_b[:, rows - rotor_rows :],
            rotor_jac,
            preferred_element_type=jnp.float32,
        )
        onward = jnp.concatenate([lam_b[:, rows - 1 :], (records * moving).astype(jnp.bfloat16)], axis=1)
        onward, lam_b, _ = lax.optimization_barrier((onward, lam_b, partials))
        onward = shifted(onward, "sector", 1)
        head = shifted(lam_b[:, :1], "sector", -1)
        lam_h = jnp.concatenate([onward[:, :1], lam_b, head], axis=1)
        picked = lam_h[:, cols]
        stator = jnp.einsum("tnkri,tnkio->tnro", picked, jac, preferred_element_type=jnp.float32)
        arrived = onward[:, 1:].astype(jnp.float32)
        rotor = records * (1.0 - moving) + arrived
        rotor_full = jnp.concatenate(
            [jnp.zeros((local_inst, rows - rotor_rows) + rotor.shape[2:], jnp.float32), rotor],
            axis=1,
        )
        base = lam + relax_wide * (rhs - (stator + rotor_full)) * live
        lam_flat, weighted = updated(got, base.reshape(-1, lanes), scale, condb)
        lam = lam_flat.reshape(shape)
    return lam


def solution(mesh):
    fine = jax.sharding.Mesh(mesh.devices.reshape(2, 4, 2, -1), INST + ("sector",))
    return jax.shard_map(
        shards,
        mesh=fine,
        in_specs=(
            P(INST, "sector", None, None),
            P(INST, "sector", None, None),
            P(INST, "sector", None),
            P("sector", None),
            P(INST, "sector", None, None, None),
            P(INST, "sector", None, None),
            P("sector", None),
            P(INST, "sector"),
            P("sector"),
        ),
        out_specs=P(INST, "sector", None, None),
        check_vma=False,
    )
```

```python
import jax
import jax.numpy as jnp
import numpy as np
from jax.experimental import pallas as pl
from jax.experimental.pallas import tpu as pltpu
from jax import lax
from jax.sharding import PartitionSpec as P

NT = 16
SWEEPS = 2


def padded(cells, sides, width):
    for axis, dim in sides:
        count = lax.axis_size(axis)
        head = lax.slice_in_dim(cells, 0, width, axis=dim)
        tail = lax.slice_in_dim(cells, cells.shape[dim] - width, cells.shape[dim], axis=dim)
        cells = jnp.concatenate(
            [
                lax.ppermute(tail, axis, [(i, (i + 1) % count) for i in range(count)]),
                cells,
                lax.ppermute(head, axis, [((i + 1) % count, i) for i in range(count)]),
            ],
            axis=dim,
        )
    return cells


def shifted(block, axis, distance):
    devices = range(lax.axis_size(axis))
    route = [((i - distance) % len(devices), i) for i in devices]
    return lax.ppermute(block, axis, route)


def spectral_matrix():
    index = jnp.arange(NT)
    offset = index[:, None] - index[None, :]
    angle = jnp.pi * offset.astype(jnp.float32) / NT
    safe_sin = jnp.where(offset == 0, jnp.float32(1.0), jnp.sin(angle))
    parity = jnp.where(offset % 2 == 0, jnp.float32(1.0), jnp.float32(-1.0))
    deriv = jnp.where(offset == 0, jnp.float32(0.0), 0.5 * parity * jnp.cos(angle) / safe_sin)
    return deriv + jnp.float32(2.0) / NT


INST = ("iy", "ix", "ic")


def routed(block, dest):
    return lax.ppermute(block, INST, [(s, dest(s)) for s in range(NT)])


def coefficient_table():
    index = np.arange(NT)
    offset = index[:, None] - index[None, :]
    angle = np.pi * offset / NT
    safe_sin = np.where(offset == 0, 1.0, np.sin(angle))
    parity = np.where(offset % 2 == 0, 1.0, -1.0)
    deriv = np.where(offset == 0, 0.0, 0.5 * parity * np.cos(angle) / safe_sin)
    dspec = deriv + 2.0 / NT
    table = np.zeros((NT, 16), np.float64)
    for s in range(NT):
        y, x, c = s // 8, (s // 2) % 4, s % 2
        members = [s, s ^ 1, s ^ 8, s ^ 9]
        targets = [y * 8 + column * 2 + c for column in range(4)]
        table[s] = [dspec[m, t] for t in targets for m in members]
    return table.astype(np.float32)


def mix_kernel(index_ref, coef_ref, own_ref, mate_ref, across_ref, diagonal_ref, o_ref):
    me = index_ref[0]
    values = (own_ref[...], mate_ref[...], across_ref[...], diagonal_ref[...])
    for slot in range(4):
        acc = coef_ref[me, slot * 4] * values[0]
        for m in range(1, 4):
            acc = acc + coef_ref[me, slot * 4 + m] * values[m]
        o_ref[slot] = acc


def partial_sums(index, own, mate, across, diagonal):
    rows, lanes = own.shape
    block = 256
    flat = pl.BlockSpec((block, lanes), lambda r, index: (r, 0))
    return pl.pallas_call(
        mix_kernel,
        grid_spec=pltpu.PrefetchScalarGridSpec(
            num_scalar_prefetch=1,
            grid=(rows // block,),
            in_specs=[pl.BlockSpec(memory_space=pltpu.SMEM), flat, flat, flat, flat],
            out_specs=pl.BlockSpec((4, block, lanes), lambda r, index: (0, r, 0)),
        ),
        out_shape=jax.ShapeDtypeStruct((4, rows, lanes), jnp.float32),
    )(index, jnp.asarray(coefficient_table()), own, mate, across, diagonal)


def update_kernel(got_ref, base_ref, scale_ref, cond_ref, lam_ref, weighted_ref):
    spec = (got_ref[0] + got_ref[1]) + (got_ref[2] + got_ref[3])
    lam = base_ref[...] - scale_ref[...] * spec
    lam_ref[...] = lam
    weighted_ref[...] = lam * cond_ref[...]


def updated(got, base, scale, condb):
    rows, lanes = base.shape
    block = 256
    flat = pl.BlockSpec((block, lanes), lambda r: (r, 0))
    return pl.pallas_call(
        update_kernel,
        grid=(rows // block,),
        in_specs=[pl.BlockSpec((4, block, lanes), lambda r: (0, r, 0)), flat, flat, flat],
        out_specs=[flat, flat],
        out_shape=[jax.ShapeDtypeStruct(base.shape, jnp.float32)] * 2,
    )(got, base, scale, condb)


def stator_kernel(cols_ref, halo_ref, jac_ref, out_ref):
    group = pl.program_id(0)
    per, width = jac_ref.shape[0], jac_ref.shape[1]
    for j in range(per):
        n = group * per + j
        acc = jnp.dot(halo_ref[cols_ref[n * width]], jac_ref[j, 0], preferred_element_type=jnp.float32)
        for k in range(1, width):
            acc = acc + jnp.dot(halo_ref[cols_ref[n * width + k]], jac_ref[j, k], preferred_element_type=jnp.float32)
        out_ref[j] = acc


def stator_of(halo, jac, cols):
    rows, width, bs, _ = jac.shape
    span, reps, lanes = halo.shape
    per = 4
    return pl.pallas_call(
        stator_kernel,
        grid_spec=pltpu.PrefetchScalarGridSpec(
            num_scalar_prefetch=1,
            grid=(rows // per,),
            in_specs=[
                pl.BlockSpec((span, reps, lanes), lambda g, cols: (0, 0, 0)),
                pl.BlockSpec((per, width, bs, bs), lambda g, cols: (g, 0, 0, 0)),
            ],
            out_specs=pl.BlockSpec((per, reps, lanes), lambda g, cols: (g, 0, 0)),
        ),
        out_shape=jax.ShapeDtypeStruct((rows, reps, lanes), jnp.float32),
    )(cols.reshape(-1), halo, jac)


def instance_mix(flat):
    i = lax.axis_index("iy") * 8 + lax.axis_index("ix") * 2 + lax.axis_index("ic")
    mate = routed(flat, lambda s: s ^ 1)
    across = routed(flat, lambda s: s ^ 8)
    diagonal = routed(across, lambda s: s ^ 1)
    partials = partial_sums(jnp.reshape(i, (1,)).astype(jnp.int32), flat, mate, across, diagonal)
    return partials, lax.all_to_all(partials, "ix", 0, 0)


def shards(lam_init, rhs, relax, cond, jac, rotor_jac, cols, rotor_shift, owned):
    local_inst = lam_init.shape[0]
    rows = lam_init.shape[1]
    rotor_rows = rotor_jac.shape[1]
    shape = lam_init.shape
    lanes = shape[-1]
    row = jnp.arange(rows)
    live = ((row >= rows - rotor_rows) | (row < owned[0])).astype(jnp.float32)[None, :, None, None]
    lam = lam_init * live
    moving = rotor_shift.astype(jnp.float32)[:, :, None, None]
    relax_wide = relax[:, :, None, :]
    cond_wide = cond[None, :, None, :]
    scale = jnp.broadcast_to(relax_wide * live, shape).reshape(-1, lanes)
    condb = jnp.broadcast_to(cond_wide, shape).reshape(-1, lanes)
    weighted = (lam * cond_wide).reshape(-1, lanes)
    scale, condb, weighted = lax.optimization_barrier((scale, condb, weighted))
    for sweep in range(SWEEPS):
        lam_b = lam.astype(jnp.bfloat16)
        partials, got = instance_mix(weighted)
        records = jnp.einsum(
            "tjri,tjio->tjro",
            lam_b[:, rows - rotor_rows :],
            rotor_jac,
            preferred_element_type=jnp.float32,
        )
        onward = jnp.concatenate([lam_b[:, rows - 1 :], (records * moving).astype(jnp.bfloat16)], axis=1)
        onward, lam_b, _ = lax.optimization_barrier((onward, lam_b, partials))
        onward = shifted(onward, "sector", 1)
        head = shifted(lam_b[:, :1], "sector", -1)
        lam_h = jnp.concatenate([onward[:, :1], lam_b, head], axis=1)
        stator = stator_of(lam_h[0], jac[0], cols)[None]
        arrived = onward[:, 1:].astype(jnp.float32)
        rotor = records * (1.0 - moving) + arrived
        rotor_full = jnp.concatenate(
            [jnp.zeros((local_inst, rows - rotor_rows) + rotor.shape[2:], jnp.float32), rotor],
            axis=1,
        )
        base = lam + relax_wide * (rhs - (stator + rotor_full)) * live
        lam_flat, weighted = updated(got, base.reshape(-1, lanes), scale, condb)
        lam = lam_flat.reshape(shape)
    return lam


def solution(mesh):
    fine = jax.sharding.Mesh(mesh.devices.reshape(2, 4, 2, -1), INST + ("sector",))
    return jax.shard_map(
        shards,
        mesh=fine,
        in_specs=(
            P(INST, "sector", None, None),
            P(INST, "sector", None, None),
            P(INST, "sector", None),
            P("sector", None),
            P(INST, "sector", None, None, None),
            P(INST, "sector", None, None),
            P("sector", None),
            P(INST, "sector"),
            P("sector"),
        ),
        out_specs=P(INST, "sector", None, None),
        check_vma=False,
    )
```

```python
import jax
import jax.numpy as jnp
import numpy as np
from jax.experimental import pallas as pl
from jax.experimental.pallas import tpu as pltpu
from jax import lax
from jax.sharding import PartitionSpec as P

NT = 16
SWEEPS = 2


def padded(cells, sides, width):
    for axis, dim in sides:
        count = lax.axis_size(axis)
        head = lax.slice_in_dim(cells, 0, width, axis=dim)
        tail = lax.slice_in_dim(cells, cells.shape[dim] - width, cells.shape[dim], axis=dim)
        cells = jnp.concatenate(
            [
                lax.ppermute(tail, axis, [(i, (i + 1) % count) for i in range(count)]),
                cells,
                lax.ppermute(head, axis, [((i + 1) % count, i) for i in range(count)]),
            ],
            axis=dim,
        )
    return cells


def shifted(block, axis, distance):
    devices = range(lax.axis_size(axis))
    route = [((i - distance) % len(devices), i) for i in devices]
    return lax.ppermute(block, axis, route)


def spectral_matrix():
    index = jnp.arange(NT)
    offset = index[:, None] - index[None, :]
    angle = jnp.pi * offset.astype(jnp.float32) / NT
    safe_sin = jnp.where(offset == 0, jnp.float32(1.0), jnp.sin(angle))
    parity = jnp.where(offset % 2 == 0, jnp.float32(1.0), jnp.float32(-1.0))
    deriv = jnp.where(offset == 0, jnp.float32(0.0), 0.5 * parity * jnp.cos(angle) / safe_sin)
    return deriv + jnp.float32(2.0) / NT


INST = ("iy", "ix", "ic")


def routed(block, dest):
    return lax.ppermute(block, INST, [(s, dest(s)) for s in range(NT)])


def coefficient_table():
    index = np.arange(NT)
    offset = index[:, None] - index[None, :]
    angle = np.pi * offset / NT
    safe_sin = np.where(offset == 0, 1.0, np.sin(angle))
    parity = np.where(offset % 2 == 0, 1.0, -1.0)
    deriv = np.where(offset == 0, 0.0, 0.5 * parity * np.cos(angle) / safe_sin)
    dspec = deriv + 2.0 / NT
    table = np.zeros((NT, 16), np.float64)
    for s in range(NT):
        y, x, c = s // 8, (s // 2) % 4, s % 2
        members = [s, s ^ 1, s ^ 8, s ^ 9]
        targets = [y * 8 + column * 2 + c for column in range(4)]
        table[s] = [dspec[m, t] for t in targets for m in members]
    return table.astype(np.float32)


def mix_kernel(index_ref, coef_ref, own_ref, mate_ref, across_ref, diagonal_ref, o_ref):
    me = index_ref[0]
    values = (own_ref[...], mate_ref[...], across_ref[...], diagonal_ref[...])
    for slot in range(4):
        acc = coef_ref[me, slot * 4] * values[0]
        for m in range(1, 4):
            acc = acc + coef_ref[me, slot * 4 + m] * values[m]
        o_ref[slot] = acc


def partial_sums(index, own, mate, across, diagonal):
    rows, lanes = own.shape
    block = 256
    flat = pl.BlockSpec((block, lanes), lambda r, index: (r, 0))
    return pl.pallas_call(
        mix_kernel,
        grid_spec=pltpu.PrefetchScalarGridSpec(
            num_scalar_prefetch=1,
            grid=(rows // block,),
            in_specs=[pl.BlockSpec(memory_space=pltpu.SMEM), flat, flat, flat, flat],
            out_specs=pl.BlockSpec((4, block, lanes), lambda r, index: (0, r, 0)),
        ),
        out_shape=jax.ShapeDtypeStruct((4, rows, lanes), jnp.float32),
    )(index, jnp.asarray(coefficient_table()), own, mate, across, diagonal)


def update_kernel(got_ref, base_ref, scale_ref, cond_ref, lam_ref, weighted_ref):
    spec = (got_ref[0] + got_ref[1]) + (got_ref[2] + got_ref[3])
    lam = base_ref[...] - scale_ref[...] * spec
    lam_ref[...] = lam
    weighted_ref[...] = lam * cond_ref[...]


def updated(got, base, scale, condb):
    rows, lanes = base.shape
    block = 256
    flat = pl.BlockSpec((block, lanes), lambda r: (r, 0))
    return pl.pallas_call(
        update_kernel,
        grid=(rows // block,),
        in_specs=[pl.BlockSpec((4, block, lanes), lambda r: (0, r, 0)), flat, flat, flat],
        out_specs=[flat, flat],
        out_shape=[jax.ShapeDtypeStruct(base.shape, jnp.float32)] * 2,
    )(got, base, scale, condb)


def instance_mix(flat):
    i = lax.axis_index("iy") * 8 + lax.axis_index("ix") * 2 + lax.axis_index("ic")
    mate = routed(flat, lambda s: s ^ 1)
    across = routed(flat, lambda s: s ^ 8)
    diagonal = routed(across, lambda s: s ^ 1)
    partials = partial_sums(jnp.reshape(i, (1,)).astype(jnp.int32), flat, mate, across, diagonal)
    return partials, lax.all_to_all(partials, "ix", 0, 0)


def shards(lam_init, rhs, relax, cond, jac, rotor_jac, cols, rotor_shift, owned):
    local_inst = lam_init.shape[0]
    rows = lam_init.shape[1]
    rotor_rows = rotor_jac.shape[1]
    shape = lam_init.shape
    lanes = shape[-1]
    row = jnp.arange(rows)
    live = ((row >= rows - rotor_rows) | (row < owned[0])).astype(jnp.float32)[None, :, None, None]
    lam = lam_init * live
    moving = rotor_shift.astype(jnp.float32)[:, :, None, None]
    relax_wide = relax[:, :, None, :]
    cond_wide = cond[None, :, None, :]
    scale = jnp.broadcast_to(relax_wide * live, shape).reshape(-1, lanes)
    condb = jnp.broadcast_to(cond_wide, shape).reshape(-1, lanes)
    weighted = (lam * cond_wide).reshape(-1, lanes)
    span = rows + 2
    edge_mask = jnp.stack([(cols == 0), (cols == span - 1)]).astype(jnp.float32)
    edge_jac = jnp.einsum("hnk,nkio->hnio", edge_mask, jac[0].astype(jnp.float32), precision=lax.Precision.HIGHEST)
    for sweep in range(SWEEPS):
        lam_b = lam.astype(jnp.bfloat16)
        partials, got = instance_mix(weighted)
        records = jnp.einsum(
            "tjri,tjio->tjro",
            lam_b[:, rows - rotor_rows :],
            rotor_jac,
            preferred_element_type=jnp.float32,
        )
        blank = jnp.zeros_like(lam_b[:, :1])
        interior = jnp.einsum(
            "tnkri,tnkio->tnro",
            jnp.concatenate([blank, lam_b, blank], axis=1)[:, cols],
            jac,
            preferred_element_type=jnp.float32,
        )
        onward = jnp.concatenate([lam_b[:, rows - 1 :], (records * moving).astype(jnp.bfloat16)], axis=1)
        onward, lam_b, interior, _ = lax.optimization_barrier((onward, lam_b, interior, partials))
        onward = shifted(onward, "sector", 1)
        head = shifted(lam_b[:, :1], "sector", -1)
        edges = jnp.concatenate([onward[:, :1], head], axis=1)[0].astype(jnp.float32)
        stator = interior + jnp.einsum("hri,hnio->nro", edges, edge_jac, precision=lax.Precision.HIGHEST)[None]
        arrived = onward[:, 1:].astype(jnp.float32)
        rotor = records * (1.0 - moving) + arrived
        rotor_full = jnp.concatenate(
            [jnp.zeros((local_inst, rows - rotor_rows) + rotor.shape[2:], jnp.float32), rotor],
            axis=1,
        )
        base = lam + relax_wide * (rhs - (stator + rotor_full)) * live
        lam_flat, weighted = updated(got, base.reshape(-1, lanes), scale, condb)
        lam = lam_flat.reshape(shape)
    return lam


def solution(mesh):
    fine = jax.sharding.Mesh(mesh.devices.reshape(2, 4, 2, -1), INST + ("sector",))
    return jax.shard_map(
        shards,
        mesh=fine,
        in_specs=(
            P(INST, "sector", None, None),
            P(INST, "sector", None, None),
            P(INST, "sector", None),
            P("sector", None),
            P(INST, "sector", None, None, None),
            P(INST, "sector", None, None),
            P("sector", None),
            P(INST, "sector"),
            P("sector"),
        ),
        out_specs=P(INST, "sector", None, None),
        check_vma=False,
    )
```

```python
import jax
import jax.numpy as jnp
import numpy as np
from jax.experimental import pallas as pl
from jax.experimental.pallas import tpu as pltpu
from jax import lax
from jax.sharding import PartitionSpec as P

NT = 16
SWEEPS = 2


def padded(cells, sides, width):
    for axis, dim in sides:
        count = lax.axis_size(axis)
        head = lax.slice_in_dim(cells, 0, width, axis=dim)
        tail = lax.slice_in_dim(cells, cells.shape[dim] - width, cells.shape[dim], axis=dim)
        cells = jnp.concatenate(
            [
                lax.ppermute(tail, axis, [(i, (i + 1) % count) for i in range(count)]),
                cells,
                lax.ppermute(head, axis, [((i + 1) % count, i) for i in range(count)]),
            ],
            axis=dim,
        )
    return cells


def shifted(block, axis, distance):
    devices = range(lax.axis_size(axis))
    route = [((i - distance) % len(devices), i) for i in devices]
    return lax.ppermute(block, axis, route)


def spectral_matrix():
    index = jnp.arange(NT)
    offset = index[:, None] - index[None, :]
    angle = jnp.pi * offset.astype(jnp.float32) / NT
    safe_sin = jnp.where(offset == 0, jnp.float32(1.0), jnp.sin(angle))
    parity = jnp.where(offset % 2 == 0, jnp.float32(1.0), jnp.float32(-1.0))
    deriv = jnp.where(offset == 0, jnp.float32(0.0), 0.5 * parity * jnp.cos(angle) / safe_sin)
    return deriv + jnp.float32(2.0) / NT


INST = ("iy", "ix", "ic")


def routed(block, dest):
    return lax.ppermute(block, INST, [(s, dest(s)) for s in range(NT)])


def coefficient_table():
    index = np.arange(NT)
    offset = index[:, None] - index[None, :]
    angle = np.pi * offset / NT
    safe_sin = np.where(offset == 0, 1.0, np.sin(angle))
    parity = np.where(offset % 2 == 0, 1.0, -1.0)
    deriv = np.where(offset == 0, 0.0, 0.5 * parity * np.cos(angle) / safe_sin)
    dspec = deriv + 2.0 / NT
    table = np.zeros((NT, 16), np.float64)
    for s in range(NT):
        y, x, c = s // 8, (s // 2) % 4, s % 2
        members = [s, s ^ 1, s ^ 8, s ^ 9]
        targets = [y * 8 + column * 2 + c for column in range(4)]
        table[s] = [dspec[m, t] for t in targets for m in members]
    return table.astype(np.float32)


def mix_kernel(index_ref, coef_ref, own_ref, mate_ref, across_ref, diagonal_ref, o_ref):
    me = index_ref[0]
    values = (own_ref[...], mate_ref[...], across_ref[...], diagonal_ref[...])
    for slot in range(4):
        acc = coef_ref[me, slot * 4] * values[0]
        for m in range(1, 4):
            acc = acc + coef_ref[me, slot * 4 + m] * values[m]
        o_ref[slot] = acc


def partial_sums(index, own, mate, across, diagonal):
    rows, lanes = own.shape
    block = 256
    flat = pl.BlockSpec((block, lanes), lambda r, index: (r, 0))
    return pl.pallas_call(
        mix_kernel,
        grid_spec=pltpu.PrefetchScalarGridSpec(
            num_scalar_prefetch=1,
            grid=(rows // block,),
            in_specs=[pl.BlockSpec(memory_space=pltpu.SMEM), flat, flat, flat, flat],
            out_specs=pl.BlockSpec((4, block, lanes), lambda r, index: (0, r, 0)),
        ),
        out_shape=jax.ShapeDtypeStruct((4, rows, lanes), jnp.float32),
    )(index, jnp.asarray(coefficient_table()), own, mate, across, diagonal)


def update_kernel(got_ref, base_ref, scale_ref, cond_ref, lam_ref, *rest):
    rows, lanes = base_ref.shape
    groups = scale_ref.shape[0]
    spec = (got_ref[0] + got_ref[1]) + (got_ref[2] + got_ref[3])
    scale = jnp.broadcast_to(scale_ref[...][:, None, :], (groups, rows // groups, lanes)).reshape(rows, lanes)
    lam = base_ref[...] - scale * spec
    lam_ref[...] = lam
    for weighted_ref in rest:
        cond = jnp.broadcast_to(cond_ref[...][:, None, :], (groups, rows // groups, lanes)).reshape(rows, lanes)
        weighted_ref[...] = lam * cond


def updated(got, base, scale, cond, outputs):
    rows, lanes = base.shape
    block = 256
    groups = block * scale.shape[0] // rows
    flat = pl.BlockSpec((block, lanes), lambda r: (r, 0))
    narrow = pl.BlockSpec((groups, lanes), lambda r: (r, 0))
    return pl.pallas_call(
        update_kernel,
        grid=(rows // block,),
        in_specs=[pl.BlockSpec((4, block, lanes), lambda r: (0, r, 0)), flat, narrow, narrow],
        out_specs=[flat] * outputs,
        out_shape=[jax.ShapeDtypeStruct(base.shape, jnp.float32)] * outputs,
    )(got, base, scale, cond)


def instance_mix(flat):
    i = lax.axis_index("iy") * 8 + lax.axis_index("ix") * 2 + lax.axis_index("ic")
    mate = routed(flat, lambda s: s ^ 1)
    across = routed(flat, lambda s: s ^ 8)
    diagonal = routed(across, lambda s: s ^ 1)
    partials = partial_sums(jnp.reshape(i, (1,)).astype(jnp.int32), flat, mate, across, diagonal)
    return partials, lax.all_to_all(partials, "ix", 0, 0)


def shards(lam_init, rhs, relax, cond, jac, rotor_jac, cols, rotor_shift, owned):
    local_inst = lam_init.shape[0]
    rows = lam_init.shape[1]
    rotor_rows = rotor_jac.shape[1]
    shape = lam_init.shape
    lanes = shape[-1]
    row = jnp.arange(rows)
    live = ((row >= rows - rotor_rows) | (row < owned[0])).astype(jnp.float32)[None, :, None, None]
    lam = lam_init * live
    moving = rotor_shift.astype(jnp.float32)[:, :, None, None]
    relax_wide = relax[:, :, None, :]
    cond_wide = cond[None, :, None, :]
    scale = relax[0] * live[0, :, 0]
    weighted = (lam * cond_wide).reshape(-1, lanes)
    for sweep in range(SWEEPS):
        lam_b = lam.astype(jnp.bfloat16)
        partials, got = instance_mix(weighted)
        records = jnp.einsum(
            "tjri,tjio->tjro",
            lam_b[:, rows - rotor_rows :],
            rotor_jac,
            preferred_element_type=jnp.float32,
        )
        onward = jnp.concatenate([lam_b[:, rows - 1 :], (records * moving).astype(jnp.bfloat16)], axis=1)
        onward, lam_b, _ = lax.optimization_barrier((onward, lam_b, partials))
        onward = shifted(onward, "sector", 1)
        head = shifted(lam_b[:, :1], "sector", -1)
        lam_h = jnp.concatenate([onward[:, :1], lam_b, head], axis=1)
        picked = lam_h[:, cols]
        stator = jnp.einsum("tnkri,tnkio->tnro", picked, jac, preferred_element_type=jnp.float32)
        arrived = onward[:, 1:].astype(jnp.float32)
        rotor = records * (1.0 - moving) + arrived
        rotor_full = jnp.concatenate(
            [jnp.zeros((local_inst, rows - rotor_rows) + rotor.shape[2:], jnp.float32), rotor],
            axis=1,
        )
        base = lam + relax_wide * (rhs - (stator + rotor_full)) * live
        fresh = updated(got, base.reshape(-1, lanes), scale, cond, 2 if sweep + 1 < SWEEPS else 1)
        lam = fresh[0].reshape(shape)
        weighted = fresh[-1]
    return lam


def solution(mesh):
    fine = jax.sharding.Mesh(mesh.devices.reshape(2, 4, 2, -1), INST + ("sector",))
    return jax.shard_map(
        shards,
        mesh=fine,
        in_specs=(
            P(INST, "sector", None, None),
            P(INST, "sector", None, None),
            P(INST, "sector", None),
            P("sector", None),
            P(INST, "sector", None, None, None),
            P(INST, "sector", None, None),
            P("sector", None),
            P(INST, "sector"),
            P("sector"),
        ),
        out_specs=P(INST, "sector", None, None),
        check_vma=False,
    )
```

```python
import jax
import jax.numpy as jnp
import numpy as np
from jax.experimental import pallas as pl
from jax.experimental.pallas import tpu as pltpu
from jax import lax
from jax.sharding import PartitionSpec as P

NT = 16
SWEEPS = 2


def padded(cells, sides, width):
    for axis, dim in sides:
        count = lax.axis_size(axis)
        head = lax.slice_in_dim(cells, 0, width, axis=dim)
        tail = lax.slice_in_dim(cells, cells.shape[dim] - width, cells.shape[dim], axis=dim)
        cells = jnp.concatenate(
            [
                lax.ppermute(tail, axis, [(i, (i + 1) % count) for i in range(count)]),
                cells,
                lax.ppermute(head, axis, [((i + 1) % count, i) for i in range(count)]),
            ],
            axis=dim,
        )
    return cells


def shifted(block, axis, distance):
    devices = range(lax.axis_size(axis))
    route = [((i - distance) % len(devices), i) for i in devices]
    return lax.ppermute(block, axis, route)


def spectral_matrix():
    index = jnp.arange(NT)
    offset = index[:, None] - index[None, :]
    angle = jnp.pi * offset.astype(jnp.float32) / NT
    safe_sin = jnp.where(offset == 0, jnp.float32(1.0), jnp.sin(angle))
    parity = jnp.where(offset % 2 == 0, jnp.float32(1.0), jnp.float32(-1.0))
    deriv = jnp.where(offset == 0, jnp.float32(0.0), 0.5 * parity * jnp.cos(angle) / safe_sin)
    return deriv + jnp.float32(2.0) / NT


INST = ("iy", "ix", "ic")


def routed(block, dest):
    return lax.ppermute(block, INST, [(s, dest(s)) for s in range(NT)])


def coefficient_table():
    index = np.arange(NT)
    offset = index[:, None] - index[None, :]
    angle = np.pi * offset / NT
    safe_sin = np.where(offset == 0, 1.0, np.sin(angle))
    parity = np.where(offset % 2 == 0, 1.0, -1.0)
    deriv = np.where(offset == 0, 0.0, 0.5 * parity * np.cos(angle) / safe_sin)
    dspec = deriv + 2.0 / NT
    table = np.zeros((NT, 16), np.float64)
    for s in range(NT):
        y, x, c = s // 8, (s // 2) % 4, s % 2
        members = [s, s ^ 1, s ^ 8, s ^ 9]
        targets = [y * 8 + column * 2 + c for column in range(4)]
        table[s] = [dspec[m, t] for t in targets for m in members]
    return table.astype(np.float32)


def mix_kernel(index_ref, coef_ref, own_ref, mate_ref, across_ref, diagonal_ref, o_ref):
    me = index_ref[0]
    coef = [[coef_ref[me, slot * 4 + m] for m in range(4)] for slot in range(4)]
    chunk = 32

    def step(c, carry):
        rows = pl.ds(pl.multiple_of(c * chunk, chunk), chunk)
        values = (own_ref[rows, :], mate_ref[rows, :], across_ref[rows, :], diagonal_ref[rows, :])
        for slot in range(4):
            acc = coef[slot][0] * values[0]
            for m in range(1, 4):
                acc = acc + coef[slot][m] * values[m]
            o_ref[slot, rows, :] = acc
        return carry

    lax.fori_loop(0, own_ref.shape[0] // chunk, step, 0, unroll=True)


def partial_sums(index, own, mate, across, diagonal):
    rows, lanes = own.shape
    block = 256
    flat = pl.BlockSpec((block, lanes), lambda r, index: (r, 0))
    return pl.pallas_call(
        mix_kernel,
        grid_spec=pltpu.PrefetchScalarGridSpec(
            num_scalar_prefetch=1,
            grid=(rows // block,),
            in_specs=[pl.BlockSpec(memory_space=pltpu.SMEM), flat, flat, flat, flat],
            out_specs=pl.BlockSpec((4, block, lanes), lambda r, index: (0, r, 0)),
        ),
        out_shape=jax.ShapeDtypeStruct((4, rows, lanes), jnp.float32),
    )(index, jnp.asarray(coefficient_table()), own, mate, across, diagonal)


def update_kernel(got_ref, base_ref, scale_ref, cond_ref, lam_ref, *rest):
    rows, lanes = base_ref.shape
    groups = scale_ref.shape[0]
    spec = (got_ref[0] + got_ref[1]) + (got_ref[2] + got_ref[3])
    scale = jnp.broadcast_to(scale_ref[...][:, None, :], (groups, rows // groups, lanes)).reshape(rows, lanes)
    lam = base_ref[...] - scale * spec
    lam_ref[...] = lam
    for weighted_ref in rest:
        cond = jnp.broadcast_to(cond_ref[...][:, None, :], (groups, rows // groups, lanes)).reshape(rows, lanes)
        weighted_ref[...] = lam * cond


def updated(got, base, scale, cond, outputs):
    rows, lanes = base.shape
    block = 256
    groups = block * scale.shape[0] // rows
    flat = pl.BlockSpec((block, lanes), lambda r: (r, 0))
    narrow = pl.BlockSpec((groups, lanes), lambda r: (r, 0))
    return pl.pallas_call(
        update_kernel,
        grid=(rows // block,),
        in_specs=[pl.BlockSpec((4, block, lanes), lambda r: (0, r, 0)), flat, narrow, narrow],
        out_specs=[flat] * outputs,
        out_shape=[jax.ShapeDtypeStruct(base.shape, jnp.float32)] * outputs,
    )(got, base, scale, cond)


def instance_mix(flat):
    i = lax.axis_index("iy") * 8 + lax.axis_index("ix") * 2 + lax.axis_index("ic")
    mate = routed(flat, lambda s: s ^ 1)
    across = routed(flat, lambda s: s ^ 8)
    diagonal = routed(across, lambda s: s ^ 1)
    partials = partial_sums(jnp.reshape(i, (1,)).astype(jnp.int32), flat, mate, across, diagonal)
    return partials, lax.all_to_all(partials, "ix", 0, 0)


def shards(lam_init, rhs, relax, cond, jac, rotor_jac, cols, rotor_shift, owned):
    local_inst = lam_init.shape[0]
    rows = lam_init.shape[1]
    rotor_rows = rotor_jac.shape[1]
    shape = lam_init.shape
    lanes = shape[-1]
    row = jnp.arange(rows)
    live = ((row >= rows - rotor_rows) | (row < owned[0])).astype(jnp.float32)[None, :, None, None]
    lam = lam_init * live
    moving = rotor_shift.astype(jnp.float32)[:, :, None, None]
    relax_wide = relax[:, :, None, :]
    cond_wide = cond[None, :, None, :]
    scale = relax[0] * live[0, :, 0]
    weighted = (lam * cond_wide).reshape(-1, lanes)
    for sweep in range(SWEEPS):
        lam_b = lam.astype(jnp.bfloat16)
        partials, got = instance_mix(weighted)
        records = jnp.einsum(
            "tjri,tjio->tjro",
            lam_b[:, rows - rotor_rows :],
            rotor_jac,
            preferred_element_type=jnp.float32,
        )
        onward = jnp.concatenate([lam_b[:, rows - 1 :], (records * moving).astype(jnp.bfloat16)], axis=1)
        onward, lam_b, _ = lax.optimization_barrier((onward, lam_b, partials))
        onward = shifted(onward, "sector", 1)
        head = shifted(lam_b[:, :1], "sector", -1)
        lam_h = jnp.concatenate([onward[:, :1], lam_b, head], axis=1)
        picked = lam_h[:, cols]
        stator = jnp.einsum("tnkri,tnkio->tnro", picked, jac, preferred_element_type=jnp.float32)
        arrived = onward[:, 1:].astype(jnp.float32)
        rotor = records * (1.0 - moving) + arrived
        rotor_full = jnp.concatenate(
            [jnp.zeros((local_inst, rows - rotor_rows) + rotor.shape[2:], jnp.float32), rotor],
            axis=1,
        )
        base = lam + relax_wide * (rhs - (stator + rotor_full)) * live
        fresh = updated(got, base.reshape(-1, lanes), scale, cond, 2 if sweep + 1 < SWEEPS else 1)
        lam = fresh[0].reshape(shape)
        weighted = fresh[-1]
    return lam


def solution(mesh):
    fine = jax.sharding.Mesh(mesh.devices.reshape(2, 4, 2, -1), INST + ("sector",))
    return jax.shard_map(
        shards,
        mesh=fine,
        in_specs=(
            P(INST, "sector", None, None),
            P(INST, "sector", None, None),
            P(INST, "sector", None),
            P("sector", None),
            P(INST, "sector", None, None, None),
            P(INST, "sector", None, None),
            P("sector", None),
            P(INST, "sector"),
            P("sector"),
        ),
        out_specs=P(INST, "sector", None, None),
        check_vma=False,
    )
```

```python
import jax
import jax.numpy as jnp
import numpy as np
from jax.experimental import pallas as pl
from jax.experimental.pallas import tpu as pltpu
from jax import lax
from jax.sharding import PartitionSpec as P

NT = 16
SWEEPS = 2


def padded(cells, sides, width):
    for axis, dim in sides:
        count = lax.axis_size(axis)
        head = lax.slice_in_dim(cells, 0, width, axis=dim)
        tail = lax.slice_in_dim(cells, cells.shape[dim] - width, cells.shape[dim], axis=dim)
        cells = jnp.concatenate(
            [
                lax.ppermute(tail, axis, [(i, (i + 1) % count) for i in range(count)]),
                cells,
                lax.ppermute(head, axis, [((i + 1) % count, i) for i in range(count)]),
            ],
            axis=dim,
        )
    return cells


def shifted(block, axis, distance):
    devices = range(lax.axis_size(axis))
    route = [((i - distance) % len(devices), i) for i in devices]
    return lax.ppermute(block, axis, route)


def spectral_matrix():
    index = jnp.arange(NT)
    offset = index[:, None] - index[None, :]
    angle = jnp.pi * offset.astype(jnp.float32) / NT
    safe_sin = jnp.where(offset == 0, jnp.float32(1.0), jnp.sin(angle))
    parity = jnp.where(offset % 2 == 0, jnp.float32(1.0), jnp.float32(-1.0))
    deriv = jnp.where(offset == 0, jnp.float32(0.0), 0.5 * parity * jnp.cos(angle) / safe_sin)
    return deriv + jnp.float32(2.0) / NT


INST = ("iy", "ix", "ic")


def routed(block, dest):
    return lax.ppermute(block, INST, [(s, dest(s)) for s in range(NT)])


def coefficient_table():
    index = np.arange(NT)
    offset = index[:, None] - index[None, :]
    angle = np.pi * offset / NT
    safe_sin = np.where(offset == 0, 1.0, np.sin(angle))
    parity = np.where(offset % 2 == 0, 1.0, -1.0)
    deriv = np.where(offset == 0, 0.0, 0.5 * parity * np.cos(angle) / safe_sin)
    dspec = deriv + 2.0 / NT
    table = np.zeros((NT, 16), np.float64)
    for s in range(NT):
        y, x, c = s // 8, (s // 2) % 4, s % 2
        members = [s, s ^ 1, s ^ 8, s ^ 9]
        targets = [y * 8 + column * 2 + c for column in range(4)]
        table[s] = [dspec[m, t] for t in targets for m in members]
    return table.astype(np.float32)


def mix_kernel(index_ref, coef_ref, own_ref, mate_ref, across_ref, diagonal_ref, o_ref):
    me = index_ref[0]
    coef = [[coef_ref[me, slot * 4 + m] for m in range(4)] for slot in range(4)]
    chunk = 32

    def step(c, carry):
        rows = pl.ds(pl.multiple_of(c * chunk, chunk), chunk)
        values = (own_ref[rows, :], mate_ref[rows, :], across_ref[rows, :], diagonal_ref[rows, :])
        for slot in range(4):
            acc = coef[slot][0] * values[0]
            for m in range(1, 4):
                acc = acc + coef[slot][m] * values[m]
            o_ref[slot, rows, :] = acc
        return carry

    lax.fori_loop(0, own_ref.shape[0] // chunk, step, 0, unroll=True)


def partial_sums(index, own, mate, across, diagonal):
    rows, lanes = own.shape
    block = rows
    flat = pl.BlockSpec((block, lanes), lambda r, index: (r, 0))
    return pl.pallas_call(
        mix_kernel,
        grid_spec=pltpu.PrefetchScalarGridSpec(
            num_scalar_prefetch=1,
            grid=(rows // block,),
            in_specs=[pl.BlockSpec(memory_space=pltpu.SMEM), flat, flat, flat, flat],
            out_specs=pl.BlockSpec((4, block, lanes), lambda r, index: (0, r, 0)),
        ),
        out_shape=jax.ShapeDtypeStruct((4, rows, lanes), jnp.float32),
    )(index, jnp.asarray(coefficient_table()), own, mate, across, diagonal)


def update_kernel(got_ref, base_ref, scale_ref, cond_ref, lam_ref, *rest):
    rows, lanes = base_ref.shape
    groups = scale_ref.shape[0]
    spec = (got_ref[0] + got_ref[1]) + (got_ref[2] + got_ref[3])
    scale = jnp.broadcast_to(scale_ref[...][:, None, :], (groups, rows // groups, lanes)).reshape(rows, lanes)
    lam = base_ref[...] - scale * spec
    lam_ref[...] = lam
    for weighted_ref in rest:
        cond = jnp.broadcast_to(cond_ref[...][:, None, :], (groups, rows // groups, lanes)).reshape(rows, lanes)
        weighted_ref[...] = lam * cond


def updated(got, base, scale, cond, outputs):
    rows, lanes = base.shape
    block = rows
    groups = block * scale.shape[0] // rows
    flat = pl.BlockSpec((block, lanes), lambda r: (r, 0))
    narrow = pl.BlockSpec((groups, lanes), lambda r: (r, 0))
    return pl.pallas_call(
        update_kernel,
        grid=(rows // block,),
        in_specs=[pl.BlockSpec((4, block, lanes), lambda r: (0, r, 0)), flat, narrow, narrow],
        out_specs=[flat] * outputs,
        out_shape=[jax.ShapeDtypeStruct(base.shape, jnp.float32)] * outputs,
    )(got, base, scale, cond)


def instance_mix(flat):
    i = lax.axis_index("iy") * 8 + lax.axis_index("ix") * 2 + lax.axis_index("ic")
    mate = routed(flat, lambda s: s ^ 1)
    across = routed(flat, lambda s: s ^ 8)
    diagonal = routed(across, lambda s: s ^ 1)
    partials = partial_sums(jnp.reshape(i, (1,)).astype(jnp.int32), flat, mate, across, diagonal)
    return partials, lax.all_to_all(partials, "ix", 0, 0)


def shards(lam_init, rhs, relax, cond, jac, rotor_jac, cols, rotor_shift, owned):
    local_inst = lam_init.shape[0]
    rows = lam_init.shape[1]
    rotor_rows = rotor_jac.shape[1]
    shape = lam_init.shape
    lanes = shape[-1]
    row = jnp.arange(rows)
    live = ((row >= rows - rotor_rows) | (row < owned[0])).astype(jnp.float32)[None, :, None, None]
    lam = lam_init * live
    moving = rotor_shift.astype(jnp.float32)[:, :, None, None]
    relax_wide = relax[:, :, None, :]
    cond_wide = cond[None, :, None, :]
    scale = relax[0] * live[0, :, 0]
    weighted = (lam * cond_wide).reshape(-1, lanes)
    for sweep in range(SWEEPS):
        lam_b = lam.astype(jnp.bfloat16)
        partials, got = instance_mix(weighted)
        records = jnp.einsum(
            "tjri,tjio->tjro",
            lam_b[:, rows - rotor_rows :],
            rotor_jac,
            preferred_element_type=jnp.float32,
        )
        onward = jnp.concatenate([lam_b[:, rows - 1 :], (records * moving).astype(jnp.bfloat16)], axis=1)
        onward, lam_b, _ = lax.optimization_barrier((onward, lam_b, partials))
        onward = shifted(onward, "sector", 1)
        head = shifted(lam_b[:, :1], "sector", -1)
        lam_h = jnp.concatenate([onward[:, :1], lam_b, head], axis=1)
        picked = lam_h[:, cols]
        stator = jnp.einsum("tnkri,tnkio->tnro", picked, jac, preferred_element_type=jnp.float32)
        arrived = onward[:, 1:].astype(jnp.float32)
        rotor = records * (1.0 - moving) + arrived
        rotor_full = jnp.concatenate(
            [jnp.zeros((local_inst, rows - rotor_rows) + rotor.shape[2:], jnp.float32), rotor],
            axis=1,
        )
        base = lam + relax_wide * (rhs - (stator + rotor_full)) * live
        fresh = updated(got, base.reshape(-1, lanes), scale, cond, 2 if sweep + 1 < SWEEPS else 1)
        lam = fresh[0].reshape(shape)
        weighted = fresh[-1]
    return lam


def solution(mesh):
    fine = jax.sharding.Mesh(mesh.devices.reshape(2, 4, 2, -1), INST + ("sector",))
    return jax.shard_map(
        shards,
        mesh=fine,
        in_specs=(
            P(INST, "sector", None, None),
            P(INST, "sector", None, None),
            P(INST, "sector", None),
            P("sector", None),
            P(INST, "sector", None, None, None),
            P(INST, "sector", None, None),
            P("sector", None),
            P(INST, "sector"),
            P("sector"),
        ),
        out_specs=P(INST, "sector", None, None),
        check_vma=False,
    )
```

```python
import jax
import jax.numpy as jnp
import numpy as np
from jax.experimental import pallas as pl
from jax.experimental.pallas import tpu as pltpu
from jax import lax
from jax.sharding import PartitionSpec as P

NT = 16
SWEEPS = 2


def padded(cells, sides, width):
    for axis, dim in sides:
        count = lax.axis_size(axis)
        head = lax.slice_in_dim(cells, 0, width, axis=dim)
        tail = lax.slice_in_dim(cells, cells.shape[dim] - width, cells.shape[dim], axis=dim)
        cells = jnp.concatenate(
            [
                lax.ppermute(tail, axis, [(i, (i + 1) % count) for i in range(count)]),
                cells,
                lax.ppermute(head, axis, [((i + 1) % count, i) for i in range(count)]),
            ],
            axis=dim,
        )
    return cells


def shifted(block, axis, distance):
    devices = range(lax.axis_size(axis))
    route = [((i - distance) % len(devices), i) for i in devices]
    return lax.ppermute(block, axis, route)


def spectral_matrix():
    index = jnp.arange(NT)
    offset = index[:, None] - index[None, :]
    angle = jnp.pi * offset.astype(jnp.float32) / NT
    safe_sin = jnp.where(offset == 0, jnp.float32(1.0), jnp.sin(angle))
    parity = jnp.where(offset % 2 == 0, jnp.float32(1.0), jnp.float32(-1.0))
    deriv = jnp.where(offset == 0, jnp.float32(0.0), 0.5 * parity * jnp.cos(angle) / safe_sin)
    return deriv + jnp.float32(2.0) / NT


INST = ("iy", "ix", "ic")


def routed(block, dest):
    return lax.ppermute(block, INST, [(s, dest(s)) for s in range(NT)])


def coefficient_table():
    index = np.arange(NT)
    offset = index[:, None] - index[None, :]
    angle = np.pi * offset / NT
    safe_sin = np.where(offset == 0, 1.0, np.sin(angle))
    parity = np.where(offset % 2 == 0, 1.0, -1.0)
    deriv = np.where(offset == 0, 0.0, 0.5 * parity * np.cos(angle) / safe_sin)
    dspec = deriv + 2.0 / NT
    table = np.zeros((NT, 16), np.float64)
    for s in range(NT):
        y, x, c = s // 8, (s // 2) % 4, s % 2
        members = [s, s ^ 1, s ^ 8, s ^ 9]
        targets = [y * 8 + column * 2 + c for column in range(4)]
        table[s] = [dspec[m, t] for t in targets for m in members]
    return table.astype(np.float32)


def mix_kernel(index_ref, coef_ref, own_ref, across_ref, pair_ref, o_ref):
    me = index_ref[0]
    coef = [[coef_ref[me, slot * 4 + m] for m in range(4)] for slot in range(4)]
    chunk = 32

    def step(c, carry):
        rows = pl.ds(pl.multiple_of(c * chunk, chunk), chunk)
        values = (own_ref[rows, :], pair_ref[0, rows, :], across_ref[rows, :], pair_ref[1, rows, :])
        for slot in range(4):
            acc = coef[slot][0] * values[0]
            for m in range(1, 4):
                acc = acc + coef[slot][m] * values[m]
            o_ref[slot, rows, :] = acc
        return carry

    lax.fori_loop(0, own_ref.shape[0] // chunk, step, 0, unroll=True)


def partial_sums(index, own, across, pair):
    rows, lanes = own.shape
    block = 256
    flat = pl.BlockSpec((block, lanes), lambda r, index: (r, 0))
    return pl.pallas_call(
        mix_kernel,
        grid_spec=pltpu.PrefetchScalarGridSpec(
            num_scalar_prefetch=1,
            grid=(rows // block,),
            in_specs=[pl.BlockSpec(memory_space=pltpu.SMEM), flat, flat, pl.BlockSpec((2, block, lanes), lambda r, index: (0, r, 0))],
            out_specs=pl.BlockSpec((4, block, lanes), lambda r, index: (0, r, 0)),
        ),
        out_shape=jax.ShapeDtypeStruct((4, rows, lanes), jnp.float32),
    )(index, jnp.asarray(coefficient_table()), own, across, pair)


def update_kernel(got_ref, base_ref, scale_ref, cond_ref, lam_ref, *rest):
    rows, lanes = base_ref.shape
    groups = scale_ref.shape[0]
    spec = (got_ref[0] + got_ref[1]) + (got_ref[2] + got_ref[3])
    scale = jnp.broadcast_to(scale_ref[...][:, None, :], (groups, rows // groups, lanes)).reshape(rows, lanes)
    lam = base_ref[...] - scale * spec
    lam_ref[...] = lam
    for weighted_ref in rest:
        cond = jnp.broadcast_to(cond_ref[...][:, None, :], (groups, rows // groups, lanes)).reshape(rows, lanes)
        weighted_ref[...] = lam * cond


def updated(got, base, scale, cond, outputs):
    rows, lanes = base.shape
    block = 256
    groups = block * scale.shape[0] // rows
    flat = pl.BlockSpec((block, lanes), lambda r: (r, 0))
    narrow = pl.BlockSpec((groups, lanes), lambda r: (r, 0))
    return pl.pallas_call(
        update_kernel,
        grid=(rows // block,),
        in_specs=[pl.BlockSpec((4, block, lanes), lambda r: (0, r, 0)), flat, narrow, narrow],
        out_specs=[flat] * outputs,
        out_shape=[jax.ShapeDtypeStruct(base.shape, jnp.float32)] * outputs,
    )(got, base, scale, cond)


def instance_mix(flat):
    i = lax.axis_index("iy") * 8 + lax.axis_index("ix") * 2 + lax.axis_index("ic")
    across = routed(flat, lambda s: s ^ 8)
    pair = routed(jnp.stack([flat, across]), lambda s: s ^ 1)
    partials = partial_sums(jnp.reshape(i, (1,)).astype(jnp.int32), flat, across, pair)
    return partials, lax.all_to_all(partials, "ix", 0, 0)


def shards(lam_init, rhs, relax, cond, jac, rotor_jac, cols, rotor_shift, owned):
    local_inst = lam_init.shape[0]
    rows = lam_init.shape[1]
    rotor_rows = rotor_jac.shape[1]
    shape = lam_init.shape
    lanes = shape[-1]
    row = jnp.arange(rows)
    live = ((row >= rows - rotor_rows) | (row < owned[0])).astype(jnp.float32)[None, :, None, None]
    lam = lam_init * live
    moving = rotor_shift.astype(jnp.float32)[:, :, None, None]
    relax_wide = relax[:, :, None, :]
    cond_wide = cond[None, :, None, :]
    scale = relax[0] * live[0, :, 0]
    weighted = (lam * cond_wide).reshape(-1, lanes)
    for sweep in range(SWEEPS):
        lam_b = lam.astype(jnp.bfloat16)
        partials, got = instance_mix(weighted)
        records = jnp.einsum(
            "tjri,tjio->tjro",
            lam_b[:, rows - rotor_rows :],
            rotor_jac,
            preferred_element_type=jnp.float32,
        )
        onward = jnp.concatenate([lam_b[:, rows - 1 :], (records * moving).astype(jnp.bfloat16)], axis=1)
        onward, lam_b, _ = lax.optimization_barrier((onward, lam_b, partials))
        onward = shifted(onward, "sector", 1)
        head = shifted(lam_b[:, :1], "sector", -1)
        lam_h = jnp.concatenate([onward[:, :1], lam_b, head], axis=1)
        picked = lam_h[:, cols]
        stator = jnp.einsum("tnkri,tnkio->tnro", picked, jac, preferred_element_type=jnp.float32)
        arrived = onward[:, 1:].astype(jnp.float32)
        rotor = records * (1.0 - moving) + arrived
        rotor_full = jnp.concatenate(
            [jnp.zeros((local_inst, rows - rotor_rows) + rotor.shape[2:], jnp.float32), rotor],
            axis=1,
        )
        base = lam + relax_wide * (rhs - (stator + rotor_full)) * live
        fresh = updated(got, base.reshape(-1, lanes), scale, cond, 2 if sweep + 1 < SWEEPS else 1)
        lam = fresh[0].reshape(shape)
        weighted = fresh[-1]
    return lam


def solution(mesh):
    fine = jax.sharding.Mesh(mesh.devices.reshape(2, 4, 2, -1), INST + ("sector",))
    return jax.shard_map(
        shards,
        mesh=fine,
        in_specs=(
            P(INST, "sector", None, None),
            P(INST, "sector", None, None),
            P(INST, "sector", None),
            P("sector", None),
            P(INST, "sector", None, None, None),
            P(INST, "sector", None, None),
            P("sector", None),
            P(INST, "sector"),
            P("sector"),
        ),
        out_specs=P(INST, "sector", None, None),
        check_vma=False,
    )
```

```python
import jax
import jax.numpy as jnp
import numpy as np
from jax.experimental import pallas as pl
from jax.experimental.pallas import tpu as pltpu
from jax import lax
from jax.sharding import PartitionSpec as P

NT = 16
SWEEPS = 2


def padded(cells, sides, width):
    for axis, dim in sides:
        count = lax.axis_size(axis)
        head = lax.slice_in_dim(cells, 0, width, axis=dim)
        tail = lax.slice_in_dim(cells, cells.shape[dim] - width, cells.shape[dim], axis=dim)
        cells = jnp.concatenate(
            [
                lax.ppermute(tail, axis, [(i, (i + 1) % count) for i in range(count)]),
                cells,
                lax.ppermute(head, axis, [((i + 1) % count, i) for i in range(count)]),
            ],
            axis=dim,
        )
    return cells


def shifted(block, axis, distance):
    devices = range(lax.axis_size(axis))
    route = [((i - distance) % len(devices), i) for i in devices]
    return lax.ppermute(block, axis, route)


def spectral_matrix():
    index = jnp.arange(NT)
    offset = index[:, None] - index[None, :]
    angle = jnp.pi * offset.astype(jnp.float32) / NT
    safe_sin = jnp.where(offset == 0, jnp.float32(1.0), jnp.sin(angle))
    parity = jnp.where(offset % 2 == 0, jnp.float32(1.0), jnp.float32(-1.0))
    deriv = jnp.where(offset == 0, jnp.float32(0.0), 0.5 * parity * jnp.cos(angle) / safe_sin)
    return deriv + jnp.float32(2.0) / NT


INST = ("iy", "ix", "ic")


def routed(block, dest):
    return lax.ppermute(block, INST, [(s, dest(s)) for s in range(NT)])


def coefficient_table():
    index = np.arange(NT)
    offset = index[:, None] - index[None, :]
    angle = np.pi * offset / NT
    safe_sin = np.where(offset == 0, 1.0, np.sin(angle))
    parity = np.where(offset % 2 == 0, 1.0, -1.0)
    deriv = np.where(offset == 0, 0.0, 0.5 * parity * np.cos(angle) / safe_sin)
    dspec = deriv + 2.0 / NT
    table = np.zeros((NT, 16), np.float64)
    for s in range(NT):
        y, x, c = s // 8, (s // 2) % 4, s % 2
        members = [s, s ^ 1, s ^ 8, s ^ 9]
        targets = [y * 8 + column * 2 + c for column in range(4)]
        table[s] = [dspec[m, t] for t in targets for m in members]
    return table.astype(np.float32)


def mix_kernel(index_ref, coef_ref, own_ref, mate_ref, across_ref, diagonal_ref, o_ref):
    me = index_ref[0]
    coef = [[coef_ref[me, slot * 4 + m] for m in range(4)] for slot in range(4)]
    chunk = 32

    def step(c, carry):
        rows = pl.ds(pl.multiple_of(c * chunk, chunk), chunk)
        values = (own_ref[rows, :], mate_ref[rows, :], across_ref[rows, :], diagonal_ref[rows, :])
        for slot in range(4):
            acc = coef[slot][0] * values[0]
            for m in range(1, 4):
                acc = acc + coef[slot][m] * values[m]
            o_ref[slot, rows, :] = acc
        return carry

    lax.fori_loop(0, own_ref.shape[0] // chunk, step, 0, unroll=True)


def partial_sums(index, own, mate, across, diagonal):
    rows, lanes = own.shape
    block = 256
    flat = pl.BlockSpec((block, lanes), lambda r, index: (r, 0))
    return pl.pallas_call(
        mix_kernel,
        grid_spec=pltpu.PrefetchScalarGridSpec(
            num_scalar_prefetch=1,
            grid=(rows // block,),
            in_specs=[pl.BlockSpec(memory_space=pltpu.SMEM), flat, flat, flat, flat],
            out_specs=pl.BlockSpec((4, block, lanes), lambda r, index: (0, r, 0)),
        ),
        out_shape=jax.ShapeDtypeStruct((4, rows, lanes), jnp.float32),
    )(index, jnp.asarray(coefficient_table()), own, mate, across, diagonal)


def update_kernel(got_ref, base_ref, scale_ref, cond_ref, lam_ref, *rest):
    rows, lanes = base_ref.shape
    groups = scale_ref.shape[0]
    spec = (got_ref[0] + got_ref[1]) + (got_ref[2] + got_ref[3])
    scale = jnp.broadcast_to(scale_ref[...][:, None, :], (groups, rows // groups, lanes)).reshape(rows, lanes)
    lam = base_ref[...] - scale * spec
    lam_ref[...] = lam
    for weighted_ref in rest:
        cond = jnp.broadcast_to(cond_ref[...][:, None, :], (groups, rows // groups, lanes)).reshape(rows, lanes)
        weighted_ref[...] = lam * cond


def updated(got, base, scale, cond, outputs):
    rows, lanes = base.shape
    block = 256
    groups = block * scale.shape[0] // rows
    flat = pl.BlockSpec((block, lanes), lambda r: (r, 0))
    narrow = pl.BlockSpec((groups, lanes), lambda r: (r, 0))
    return pl.pallas_call(
        update_kernel,
        grid=(rows // block,),
        in_specs=[pl.BlockSpec((4, block, lanes), lambda r: (0, r, 0)), flat, narrow, narrow],
        out_specs=[flat] * outputs,
        out_shape=[jax.ShapeDtypeStruct(base.shape, jnp.float32)] * outputs,
    )(got, base, scale, cond)


def instance_mix(flat, hold=None):
    i = lax.axis_index("iy") * 8 + lax.axis_index("ix") * 2 + lax.axis_index("ic")
    mate = routed(flat, lambda s: s ^ 1)
    across = routed(flat, lambda s: s ^ 8)
    if hold is not None:
        across = lax.optimization_barrier((across, hold))[0]
    diagonal = routed(across, lambda s: s ^ 1)
    partials = partial_sums(jnp.reshape(i, (1,)).astype(jnp.int32), flat, mate, across, diagonal)
    return partials, lax.all_to_all(partials, "ix", 0, 0)


def shards(lam_init, rhs, relax, cond, jac, rotor_jac, cols, rotor_shift, owned):
    local_inst = lam_init.shape[0]
    rows = lam_init.shape[1]
    rotor_rows = rotor_jac.shape[1]
    shape = lam_init.shape
    lanes = shape[-1]
    row = jnp.arange(rows)
    live = ((row >= rows - rotor_rows) | (row < owned[0])).astype(jnp.float32)[None, :, None, None]
    lam = lam_init * live
    moving = rotor_shift.astype(jnp.float32)[:, :, None, None]
    relax_wide = relax[:, :, None, :]
    cond_wide = cond[None, :, None, :]
    scale = relax[0] * live[0, :, 0]
    weighted = (lam * cond_wide).reshape(-1, lanes)
    for sweep in range(SWEEPS):
        lam_b = lam.astype(jnp.bfloat16)
        records = jnp.einsum(
            "tjri,tjio->tjro",
            lam_b[:, rows - rotor_rows :],
            rotor_jac,
            preferred_element_type=jnp.float32,
        )
        onward = jnp.concatenate([lam_b[:, rows - 1 :], (records * moving).astype(jnp.bfloat16)], axis=1)
        if sweep == 0:
            partials, got = instance_mix(weighted)
            onward, lam_b, _ = lax.optimization_barrier((onward, lam_b, partials))
            onward = shifted(onward, "sector", 1)
            head = shifted(lam_b[:, :1], "sector", -1)
        else:
            onward = shifted(onward, "sector", 1)
            head = shifted(lam_b[:, :1], "sector", -1)
            partials, got = instance_mix(weighted, (onward, head))
        lam_h = jnp.concatenate([onward[:, :1], lam_b, head], axis=1)
        picked = lam_h[:, cols]
        stator = jnp.einsum("tnkri,tnkio->tnro", picked, jac, preferred_element_type=jnp.float32)
        arrived = onward[:, 1:].astype(jnp.float32)
        rotor = records * (1.0 - moving) + arrived
        rotor_full = jnp.concatenate(
            [jnp.zeros((local_inst, rows - rotor_rows) + rotor.shape[2:], jnp.float32), rotor],
            axis=1,
        )
        base = lam + relax_wide * (rhs - (stator + rotor_full)) * live
        fresh = updated(got, base.reshape(-1, lanes), scale, cond, 2 if sweep + 1 < SWEEPS else 1)
        lam = fresh[0].reshape(shape)
        weighted = fresh[-1]
    return lam


def solution(mesh):
    fine = jax.sharding.Mesh(mesh.devices.reshape(2, 4, 2, -1), INST + ("sector",))
    return jax.shard_map(
        shards,
        mesh=fine,
        in_specs=(
            P(INST, "sector", None, None),
            P(INST, "sector", None, None),
            P(INST, "sector", None),
            P("sector", None),
            P(INST, "sector", None, None, None),
            P(INST, "sector", None, None),
            P("sector", None),
            P(INST, "sector"),
            P("sector"),
        ),
        out_specs=P(INST, "sector", None, None),
        check_vma=False,
    )
```

```python
import jax
import jax.numpy as jnp
import numpy as np
from jax.experimental import pallas as pl
from jax.experimental.pallas import tpu as pltpu
from jax import lax
from jax.sharding import PartitionSpec as P

NT = 16
SWEEPS = 2


def padded(cells, sides, width):
    for axis, dim in sides:
        count = lax.axis_size(axis)
        head = lax.slice_in_dim(cells, 0, width, axis=dim)
        tail = lax.slice_in_dim(cells, cells.shape[dim] - width, cells.shape[dim], axis=dim)
        cells = jnp.concatenate(
            [
                lax.ppermute(tail, axis, [(i, (i + 1) % count) for i in range(count)]),
                cells,
                lax.ppermute(head, axis, [((i + 1) % count, i) for i in range(count)]),
            ],
            axis=dim,
        )
    return cells


def shifted(block, axis, distance):
    devices = range(lax.axis_size(axis))
    route = [((i - distance) % len(devices), i) for i in devices]
    return lax.ppermute(block, axis, route)


def spectral_matrix():
    index = jnp.arange(NT)
    offset = index[:, None] - index[None, :]
    angle = jnp.pi * offset.astype(jnp.float32) / NT
    safe_sin = jnp.where(offset == 0, jnp.float32(1.0), jnp.sin(angle))
    parity = jnp.where(offset % 2 == 0, jnp.float32(1.0), jnp.float32(-1.0))
    deriv = jnp.where(offset == 0, jnp.float32(0.0), 0.5 * parity * jnp.cos(angle) / safe_sin)
    return deriv + jnp.float32(2.0) / NT


INST = ("iy", "ix", "ic")


def routed(block, dest):
    return lax.ppermute(block, INST, [(s, dest(s)) for s in range(NT)])


def coefficient_table():
    index = np.arange(NT)
    offset = index[:, None] - index[None, :]
    angle = np.pi * offset / NT
    safe_sin = np.where(offset == 0, 1.0, np.sin(angle))
    parity = np.where(offset % 2 == 0, 1.0, -1.0)
    deriv = np.where(offset == 0, 0.0, 0.5 * parity * np.cos(angle) / safe_sin)
    dspec = deriv + 2.0 / NT
    table = np.zeros((NT, 16), np.float64)
    for s in range(NT):
        y, x, c = s // 8, (s // 2) % 4, s % 2
        members = [s, s ^ 1, s ^ 8, s ^ 9]
        targets = [y * 8 + column * 2 + c for column in range(4)]
        table[s] = [dspec[m, t] for t in targets for m in members]
    return table.astype(np.float32)


def mix_kernel(index_ref, coef_ref, own_ref, mate_ref, across_ref, diagonal_ref, o_ref):
    me = index_ref[0]
    coef = [[coef_ref[me, slot * 4 + m] for m in range(4)] for slot in range(4)]
    chunk = 32

    def step(c, carry):
        rows = pl.ds(pl.multiple_of(c * chunk, chunk), chunk)
        values = (own_ref[rows, :], mate_ref[rows, :], across_ref[rows, :], diagonal_ref[rows, :])
        for slot in range(4):
            acc = coef[slot][0] * values[0]
            for m in range(1, 4):
                acc = acc + coef[slot][m] * values[m]
            o_ref[slot, rows, :] = acc
        return carry

    lax.fori_loop(0, own_ref.shape[0] // chunk, step, 0, unroll=True)


def partial_sums(index, own, mate, across, diagonal):
    rows, lanes = own.shape
    block = 256
    flat = pl.BlockSpec((block, lanes), lambda r, index: (r, 0))
    return pl.pallas_call(
        mix_kernel,
        grid_spec=pltpu.PrefetchScalarGridSpec(
            num_scalar_prefetch=1,
            grid=(rows // block,),
            in_specs=[pl.BlockSpec(memory_space=pltpu.SMEM), flat, flat, flat, flat],
            out_specs=pl.BlockSpec((4, block, lanes), lambda r, index: (0, r, 0)),
        ),
        out_shape=jax.ShapeDtypeStruct((4, rows, lanes), jnp.float32),
    )(index, jnp.asarray(coefficient_table()), own, mate, across, diagonal)


def update_kernel(got_ref, base_ref, scale_ref, cond_ref, lam_ref, *rest):
    rows, lanes = base_ref.shape
    groups = scale_ref.shape[0]
    spec = (got_ref[0] + got_ref[1]) + (got_ref[2] + got_ref[3])
    scale = jnp.broadcast_to(scale_ref[...][:, None, :], (groups, rows // groups, lanes)).reshape(rows, lanes)
    lam = base_ref[...] - scale * spec
    lam_ref[...] = lam
    for weighted_ref in rest:
        cond = jnp.broadcast_to(cond_ref[...][:, None, :], (groups, rows // groups, lanes)).reshape(rows, lanes)
        weighted_ref[...] = lam * cond


def updated(got, base, scale, cond, outputs):
    rows, lanes = base.shape
    block = 256
    groups = block * scale.shape[0] // rows
    flat = pl.BlockSpec((block, lanes), lambda r: (r, 0))
    narrow = pl.BlockSpec((groups, lanes), lambda r: (r, 0))
    return pl.pallas_call(
        update_kernel,
        grid=(rows // block,),
        in_specs=[pl.BlockSpec((4, block, lanes), lambda r: (0, r, 0)), flat, narrow, narrow],
        out_specs=[flat] * outputs,
        out_shape=[jax.ShapeDtypeStruct(base.shape, jnp.float32)] * outputs,
    )(got, base, scale, cond)


def instance_mix(flat):
    i = lax.axis_index("iy") * 8 + lax.axis_index("ix") * 2 + lax.axis_index("ic")
    mate = routed(flat, lambda s: s ^ 1)
    across = routed(flat, lambda s: s ^ 8)
    diagonal = routed(across, lambda s: s ^ 1)
    partials = partial_sums(jnp.reshape(i, (1,)).astype(jnp.int32), flat, mate, across, diagonal)
    return partials, lax.all_to_all(partials, "ix", 0, 0)


def shards(lam_init, rhs, relax, cond, jac, rotor_jac, cols, rotor_shift, owned):
    local_inst = lam_init.shape[0]
    rows = lam_init.shape[1]
    rotor_rows = rotor_jac.shape[1]
    shape = lam_init.shape
    lanes = shape[-1]
    row = jnp.arange(rows)
    live = ((row >= rows - rotor_rows) | (row < owned[0])).astype(jnp.float32)[None, :, None, None]
    lam = lam_init * live
    moving = rotor_shift.astype(jnp.float32)[:, :, None, None]
    relax_wide = relax[:, :, None, :]
    cond_wide = cond[None, :, None, :]
    scale = relax[0] * live[0, :, 0]
    weighted = (lam * cond_wide).reshape(-1, lanes)
    select = (cols[:, :, None] == jnp.arange(rows + 2)[None, None, :]).astype(jnp.bfloat16)
    for sweep in range(SWEEPS):
        lam_b = lam.astype(jnp.bfloat16)
        partials, got = instance_mix(weighted)
        records = jnp.einsum(
            "tjri,tjio->tjro",
            lam_b[:, rows - rotor_rows :],
            rotor_jac,
            preferred_element_type=jnp.float32,
        )
        onward = jnp.concatenate([lam_b[:, rows - 1 :], (records * moving).astype(jnp.bfloat16)], axis=1)
        onward, lam_b, _ = lax.optimization_barrier((onward, lam_b, partials))
        onward = shifted(onward, "sector", 1)
        head = shifted(lam_b[:, :1], "sector", -1)
        lam_h = jnp.concatenate([onward[:, :1], lam_b, head], axis=1)
        picked = jnp.einsum("nkm,tmri->tnkri", select, lam_h, preferred_element_type=jnp.float32).astype(jnp.bfloat16)
        stator = jnp.einsum("tnkri,tnkio->tnro", picked, jac, preferred_element_type=jnp.float32)
        arrived = onward[:, 1:].astype(jnp.float32)
        rotor = records * (1.0 - moving) + arrived
        rotor_full = jnp.concatenate(
            [jnp.zeros((local_inst, rows - rotor_rows) + rotor.shape[2:], jnp.float32), rotor],
            axis=1,
        )
        base = lam + relax_wide * (rhs - (stator + rotor_full)) * live
        fresh = updated(got, base.reshape(-1, lanes), scale, cond, 2 if sweep + 1 < SWEEPS else 1)
        lam = fresh[0].reshape(shape)
        weighted = fresh[-1]
    return lam


def solution(mesh):
    fine = jax.sharding.Mesh(mesh.devices.reshape(2, 4, 2, -1), INST + ("sector",))
    return jax.shard_map(
        shards,
        mesh=fine,
        in_specs=(
            P(INST, "sector", None, None),
            P(INST, "sector", None, None),
            P(INST, "sector", None),
            P("sector", None),
            P(INST, "sector", None, None, None),
            P(INST, "sector", None, None),
            P("sector", None),
            P(INST, "sector"),
            P("sector"),
        ),
        out_specs=P(INST, "sector", None, None),
        check_vma=False,
    )
```

```python
import jax
import jax.numpy as jnp
import numpy as np
from jax.experimental import pallas as pl
from jax.experimental.pallas import tpu as pltpu
from jax import lax
from jax.sharding import PartitionSpec as P

NT = 16
SWEEPS = 2


def padded(cells, sides, width):
    for axis, dim in sides:
        count = lax.axis_size(axis)
        head = lax.slice_in_dim(cells, 0, width, axis=dim)
        tail = lax.slice_in_dim(cells, cells.shape[dim] - width, cells.shape[dim], axis=dim)
        cells = jnp.concatenate(
            [
                lax.ppermute(tail, axis, [(i, (i + 1) % count) for i in range(count)]),
                cells,
                lax.ppermute(head, axis, [((i + 1) % count, i) for i in range(count)]),
            ],
            axis=dim,
        )
    return cells


def shifted(block, axis, distance):
    devices = range(lax.axis_size(axis))
    route = [((i - distance) % len(devices), i) for i in devices]
    return lax.ppermute(block, axis, route)


def spectral_matrix():
    index = jnp.arange(NT)
    offset = index[:, None] - index[None, :]
    angle = jnp.pi * offset.astype(jnp.float32) / NT
    safe_sin = jnp.where(offset == 0, jnp.float32(1.0), jnp.sin(angle))
    parity = jnp.where(offset % 2 == 0, jnp.float32(1.0), jnp.float32(-1.0))
    deriv = jnp.where(offset == 0, jnp.float32(0.0), 0.5 * parity * jnp.cos(angle) / safe_sin)
    return deriv + jnp.float32(2.0) / NT


INST = ("iy", "ix", "ic")


def routed(block, dest):
    return lax.ppermute(block, INST, [(s, dest(s)) for s in range(NT)])


def coefficient_table():
    index = np.arange(NT)
    offset = index[:, None] - index[None, :]
    angle = np.pi * offset / NT
    safe_sin = np.where(offset == 0, 1.0, np.sin(angle))
    parity = np.where(offset % 2 == 0, 1.0, -1.0)
    deriv = np.where(offset == 0, 0.0, 0.5 * parity * np.cos(angle) / safe_sin)
    dspec = deriv + 2.0 / NT
    table = np.zeros((NT, 16), np.float64)
    for s in range(NT):
        y, x, c = s // 8, (s // 2) % 4, s % 2
        members = [s, s ^ 1, s ^ 8, s ^ 9]
        targets = [y * 8 + column * 2 + c for column in range(4)]
        table[s] = [dspec[m, t] for t in targets for m in members]
    return table.astype(np.float32)


def mix_kernel(index_ref, coef_ref, own_ref, mate_ref, across_ref, diagonal_ref, o_ref):
    me = index_ref[0]
    coef = [[coef_ref[me, slot * 4 + m] for m in range(4)] for slot in range(4)]
    chunk = 32

    def step(c, carry):
        rows = pl.ds(pl.multiple_of(c * chunk, chunk), chunk)
        values = (own_ref[rows, :], mate_ref[rows, :], across_ref[rows, :], diagonal_ref[rows, :])
        for slot in range(4):
            acc = coef[slot][0] * values[0]
            for m in range(1, 4):
                acc = acc + coef[slot][m] * values[m]
            o_ref[slot, rows, :] = acc
        return carry

    lax.fori_loop(0, own_ref.shape[0] // chunk, step, 0, unroll=True)


def partial_sums(index, own, mate, across, diagonal):
    rows, lanes = own.shape
    block = 256
    flat = pl.BlockSpec((block, lanes), lambda r, index: (r, 0))
    return pl.pallas_call(
        mix_kernel,
        grid_spec=pltpu.PrefetchScalarGridSpec(
            num_scalar_prefetch=1,
            grid=(rows // block,),
            in_specs=[pl.BlockSpec(memory_space=pltpu.SMEM), flat, flat, flat, flat],
            out_specs=pl.BlockSpec((4, block, lanes), lambda r, index: (0, r, 0)),
        ),
        out_shape=jax.ShapeDtypeStruct((4, rows, lanes), jnp.float32),
    )(index, jnp.asarray(coefficient_table()), own, mate, across, diagonal)


def update_kernel(got_ref, base_ref, scale_ref, cond_ref, lam_ref, *rest):
    rows, lanes = base_ref.shape
    groups = scale_ref.shape[0]
    spec = (got_ref[0] + got_ref[1]) + (got_ref[2] + got_ref[3])
    scale = jnp.broadcast_to(scale_ref[...][:, None, :], (groups, rows // groups, lanes)).reshape(rows, lanes)
    lam = base_ref[...] - scale * spec
    lam_ref[...] = lam
    for weighted_ref in rest:
        cond = jnp.broadcast_to(cond_ref[...][:, None, :], (groups, rows // groups, lanes)).reshape(rows, lanes)
        weighted_ref[...] = lam * cond


def updated(got, base, scale, cond, outputs):
    rows, lanes = base.shape
    block = 256
    groups = block * scale.shape[0] // rows
    flat = pl.BlockSpec((block, lanes), lambda r: (r, 0))
    narrow = pl.BlockSpec((groups, lanes), lambda r: (r, 0))
    return pl.pallas_call(
        update_kernel,
        grid=(rows // block,),
        in_specs=[pl.BlockSpec((4, block, lanes), lambda r: (0, r, 0)), flat, narrow, narrow],
        out_specs=[flat] * outputs,
        out_shape=[jax.ShapeDtypeStruct(base.shape, jnp.float32)] * outputs,
    )(got, base, scale, cond)


def instance_mix(flat):
    i = lax.axis_index("iy") * 8 + lax.axis_index("ix") * 2 + lax.axis_index("ic")
    mate = routed(flat, lambda s: s ^ 1)
    across = routed(flat, lambda s: s ^ 8)
    diagonal = routed(across, lambda s: s ^ 1)
    partials = partial_sums(jnp.reshape(i, (1,)).astype(jnp.int32), flat, mate, across, diagonal)
    return partials, lax.all_to_all(partials, "ix", 0, 0)


def shards(lam_init, rhs, relax, cond, jac, rotor_jac, cols, rotor_shift, owned):
    local_inst = lam_init.shape[0]
    rows = lam_init.shape[1]
    rotor_rows = rotor_jac.shape[1]
    shape = lam_init.shape
    lanes = shape[-1]
    row = jnp.arange(rows)
    live = ((row >= rows - rotor_rows) | (row < owned[0])).astype(jnp.float32)[None, :, None, None]
    lam = lam_init * live
    moving = rotor_shift.astype(jnp.float32)[:, :, None, None]
    relax_wide = relax[:, :, None, :]
    cond_wide = cond[None, :, None, :]
    scale = relax[0] * live[0, :, 0]
    weighted = (lam_init * (live * cond_wide)).reshape(-1, lanes)
    lam = lax.optimization_barrier((lam_init, weighted))[0] * live
    for sweep in range(SWEEPS):
        lam_b = lam.astype(jnp.bfloat16)
        partials, got = instance_mix(weighted)
        records = jnp.einsum(
            "tjri,tjio->tjro",
            lam_b[:, rows - rotor_rows :],
            rotor_jac,
            preferred_element_type=jnp.float32,
        )
        onward = jnp.concatenate([lam_b[:, rows - 1 :], (records * moving).astype(jnp.bfloat16)], axis=1)
        onward, lam_b, _ = lax.optimization_barrier((onward, lam_b, partials))
        onward = shifted(onward, "sector", 1)
        head = shifted(lam_b[:, :1], "sector", -1)
        lam_h = jnp.concatenate([onward[:, :1], lam_b, head], axis=1)
        picked = lam_h[:, cols]
        stator = jnp.einsum("tnkri,tnkio->tnro", picked, jac, preferred_element_type=jnp.float32)
        arrived = onward[:, 1:].astype(jnp.float32)
        rotor = records * (1.0 - moving) + arrived
        rotor_full = jnp.concatenate(
            [jnp.zeros((local_inst, rows - rotor_rows) + rotor.shape[2:], jnp.float32), rotor],
            axis=1,
        )
        base = lam + relax_wide * (rhs - (stator + rotor_full)) * live
        fresh = updated(got, base.reshape(-1, lanes), scale, cond, 2 if sweep + 1 < SWEEPS else 1)
        lam = fresh[0].reshape(shape)
        weighted = fresh[-1]
    return lam


def solution(mesh):
    fine = jax.sharding.Mesh(mesh.devices.reshape(2, 4, 2, -1), INST + ("sector",))
    return jax.shard_map(
        shards,
        mesh=fine,
        in_specs=(
            P(INST, "sector", None, None),
            P(INST, "sector", None, None),
            P(INST, "sector", None),
            P("sector", None),
            P(INST, "sector", None, None, None),
            P(INST, "sector", None, None),
            P("sector", None),
            P(INST, "sector"),
            P("sector"),
        ),
        out_specs=P(INST, "sector", None, None),
        check_vma=False,
    )
```

```python
import jax
import jax.numpy as jnp
import numpy as np
from jax.experimental import pallas as pl
from jax.experimental.pallas import tpu as pltpu
from jax import lax
from jax.sharding import PartitionSpec as P

NT = 16
SWEEPS = 2


def padded(cells, sides, width):
    for axis, dim in sides:
        count = lax.axis_size(axis)
        head = lax.slice_in_dim(cells, 0, width, axis=dim)
        tail = lax.slice_in_dim(cells, cells.shape[dim] - width, cells.shape[dim], axis=dim)
        cells = jnp.concatenate(
            [
                lax.ppermute(tail, axis, [(i, (i + 1) % count) for i in range(count)]),
                cells,
                lax.ppermute(head, axis, [((i + 1) % count, i) for i in range(count)]),
            ],
            axis=dim,
        )
    return cells


def shifted(block, axis, distance):
    devices = range(lax.axis_size(axis))
    route = [((i - distance) % len(devices), i) for i in devices]
    return lax.ppermute(block, axis, route)


def spectral_matrix():
    index = jnp.arange(NT)
    offset = index[:, None] - index[None, :]
    angle = jnp.pi * offset.astype(jnp.float32) / NT
    safe_sin = jnp.where(offset == 0, jnp.float32(1.0), jnp.sin(angle))
    parity = jnp.where(offset % 2 == 0, jnp.float32(1.0), jnp.float32(-1.0))
    deriv = jnp.where(offset == 0, jnp.float32(0.0), 0.5 * parity * jnp.cos(angle) / safe_sin)
    return deriv + jnp.float32(2.0) / NT


INST = ("iy", "ix", "ic")


def routed(block, dest):
    return lax.ppermute(block, INST, [(s, dest(s)) for s in range(NT)])


def coefficient_table():
    index = np.arange(NT)
    offset = index[:, None] - index[None, :]
    angle = np.pi * offset / NT
    safe_sin = np.where(offset == 0, 1.0, np.sin(angle))
    parity = np.where(offset % 2 == 0, 1.0, -1.0)
    deriv = np.where(offset == 0, 0.0, 0.5 * parity * np.cos(angle) / safe_sin)
    dspec = deriv + 2.0 / NT
    table = np.zeros((NT, 16), np.float64)
    for s in range(NT):
        y, x, c = s // 8, (s // 2) % 4, s % 2
        members = [s, s ^ 1, s ^ 8, s ^ 9]
        targets = [y * 8 + column * 2 + c for column in range(4)]
        table[s] = [dspec[m, t] for t in targets for m in members]
    return table.astype(np.float32)


def mix_kernel(index_ref, coef_ref, own_ref, mate_ref, across_ref, diagonal_ref, o_ref):
    me = index_ref[0]
    coef = [[coef_ref[me, slot * 4 + m] for m in range(4)] for slot in range(4)]
    chunk = 32

    def step(c, carry):
        rows = pl.ds(pl.multiple_of(c * chunk, chunk), chunk)
        values = (own_ref[rows, :], mate_ref[rows, :], across_ref[rows, :], diagonal_ref[rows, :])
        for slot in range(4):
            acc = coef[slot][0] * values[0]
            for m in range(1, 4):
                acc = acc + coef[slot][m] * values[m]
            o_ref[slot, rows, :] = acc
        return carry

    lax.fori_loop(0, own_ref.shape[0] // chunk, step, 0, unroll=True)


def partial_sums(index, own, mate, across, diagonal):
    rows, lanes = own.shape
    block = 256
    flat = pl.BlockSpec((block, lanes), lambda r, index: (r, 0))
    return pl.pallas_call(
        mix_kernel,
        grid_spec=pltpu.PrefetchScalarGridSpec(
            num_scalar_prefetch=1,
            grid=(rows // block,),
            in_specs=[pl.BlockSpec(memory_space=pltpu.SMEM), flat, flat, flat, flat],
            out_specs=pl.BlockSpec((4, block, lanes), lambda r, index: (0, r, 0)),
        ),
        out_shape=jax.ShapeDtypeStruct((4, rows, lanes), jnp.float32),
    )(index, jnp.asarray(coefficient_table()), own, mate, across, diagonal)


def update_kernel(got_ref, lam_ref, rhs_ref, local_ref, scale_ref, cond_ref, out_ref, *rest):
    rows, lanes = lam_ref.shape
    groups = scale_ref.shape[0]
    spec = (got_ref[0] + got_ref[1]) + (got_ref[2] + got_ref[3])
    scale = jnp.broadcast_to(scale_ref[...][:, None, :], (groups, rows // groups, lanes)).reshape(rows, lanes)
    lam = lam_ref[...] + scale * (rhs_ref[...] - (local_ref[...] + spec))
    out_ref[...] = lam
    for weighted_ref in rest:
        cond = jnp.broadcast_to(cond_ref[...][:, None, :], (groups, rows // groups, lanes)).reshape(rows, lanes)
        weighted_ref[...] = lam * cond


def updated(got, lam, rhs, local, scale, cond, outputs):
    rows, lanes = lam.shape
    block = 256
    groups = block * scale.shape[0] // rows
    flat = pl.BlockSpec((block, lanes), lambda r: (r, 0))
    narrow = pl.BlockSpec((groups, lanes), lambda r: (r, 0))
    return pl.pallas_call(
        update_kernel,
        grid=(rows // block,),
        in_specs=[pl.BlockSpec((4, block, lanes), lambda r: (0, r, 0)), flat, flat, flat, narrow, narrow],
        out_specs=[flat] * outputs,
        out_shape=[jax.ShapeDtypeStruct(lam.shape, jnp.float32)] * outputs,
    )(got, lam, rhs, local, scale, cond)


def instance_mix(flat):
    i = lax.axis_index("iy") * 8 + lax.axis_index("ix") * 2 + lax.axis_index("ic")
    mate = routed(flat, lambda s: s ^ 1)
    across = routed(flat, lambda s: s ^ 8)
    diagonal = routed(across, lambda s: s ^ 1)
    partials = partial_sums(jnp.reshape(i, (1,)).astype(jnp.int32), flat, mate, across, diagonal)
    return partials, lax.all_to_all(partials, "ix", 0, 0)


def shards(lam_init, rhs, relax, cond, jac, rotor_jac, cols, rotor_shift, owned):
    local_inst = lam_init.shape[0]
    rows = lam_init.shape[1]
    rotor_rows = rotor_jac.shape[1]
    shape = lam_init.shape
    lanes = shape[-1]
    row = jnp.arange(rows)
    live = ((row >= rows - rotor_rows) | (row < owned[0])).astype(jnp.float32)[None, :, None, None]
    lam = lam_init * live
    moving = rotor_shift.astype(jnp.float32)[:, :, None, None]
    relax_wide = relax[:, :, None, :]
    cond_wide = cond[None, :, None, :]
    scale = relax[0] * live[0, :, 0]
    weighted = (lam * cond_wide).reshape(-1, lanes)
    for sweep in range(SWEEPS):
        lam_b = lam.astype(jnp.bfloat16)
        partials, got = instance_mix(weighted)
        records = jnp.einsum(
            "tjri,tjio->tjro",
            lam_b[:, rows - rotor_rows :],
            rotor_jac,
            preferred_element_type=jnp.float32,
        )
        onward = jnp.concatenate([lam_b[:, rows - 1 :], (records * moving).astype(jnp.bfloat16)], axis=1)
        onward, lam_b, _ = lax.optimization_barrier((onward, lam_b, partials))
        onward = shifted(onward, "sector", 1)
        head = shifted(lam_b[:, :1], "sector", -1)
        lam_h = jnp.concatenate([onward[:, :1], lam_b, head], axis=1)
        picked = lam_h[:, cols]
        stator = jnp.einsum("tnkri,tnkio->tnro", picked, jac, preferred_element_type=jnp.float32)
        arrived = onward[:, 1:].astype(jnp.float32)
        rotor = records * (1.0 - moving) + arrived
        rotor_full = jnp.concatenate(
            [jnp.zeros((local_inst, rows - rotor_rows) + rotor.shape[2:], jnp.float32), rotor],
            axis=1,
        )
        local = (stator + rotor_full).reshape(-1, lanes)
        fresh = updated(
            got, lam.reshape(-1, lanes), rhs.reshape(-1, lanes), local, scale, cond, 2 if sweep + 1 < SWEEPS else 1
        )
        lam = fresh[0].reshape(shape)
        weighted = fresh[-1]
    return lam


def solution(mesh):
    fine = jax.sharding.Mesh(mesh.devices.reshape(2, 4, 2, -1), INST + ("sector",))
    return jax.shard_map(
        shards,
        mesh=fine,
        in_specs=(
            P(INST, "sector", None, None),
            P(INST, "sector", None, None),
            P(INST, "sector", None),
            P("sector", None),
            P(INST, "sector", None, None, None),
            P(INST, "sector", None, None),
            P("sector", None),
            P(INST, "sector"),
            P("sector"),
        ),
        out_specs=P(INST, "sector", None, None),
        check_vma=False,
    )
```

```python
import jax
import jax.numpy as jnp
import numpy as np
from jax.experimental import pallas as pl
from jax.experimental.pallas import tpu as pltpu
from jax import lax
from jax.sharding import PartitionSpec as P

NT = 16
SWEEPS = 2


def padded(cells, sides, width):
    for axis, dim in sides:
        count = lax.axis_size(axis)
        head = lax.slice_in_dim(cells, 0, width, axis=dim)
        tail = lax.slice_in_dim(cells, cells.shape[dim] - width, cells.shape[dim], axis=dim)
        cells = jnp.concatenate(
            [
                lax.ppermute(tail, axis, [(i, (i + 1) % count) for i in range(count)]),
                cells,
                lax.ppermute(head, axis, [((i + 1) % count, i) for i in range(count)]),
            ],
            axis=dim,
        )
    return cells


def shifted(block, axis, distance):
    devices = range(lax.axis_size(axis))
    route = [((i - distance) % len(devices), i) for i in devices]
    return lax.ppermute(block, axis, route)


def spectral_matrix():
    index = jnp.arange(NT)
    offset = index[:, None] - index[None, :]
    angle = jnp.pi * offset.astype(jnp.float32) / NT
    safe_sin = jnp.where(offset == 0, jnp.float32(1.0), jnp.sin(angle))
    parity = jnp.where(offset % 2 == 0, jnp.float32(1.0), jnp.float32(-1.0))
    deriv = jnp.where(offset == 0, jnp.float32(0.0), 0.5 * parity * jnp.cos(angle) / safe_sin)
    return deriv + jnp.float32(2.0) / NT


INST = ("iy", "ix", "ic")


def routed(block, dest):
    return lax.ppermute(block, INST, [(s, dest(s)) for s in range(NT)])


def coefficient_table():
    index = np.arange(NT)
    offset = index[:, None] - index[None, :]
    angle = np.pi * offset / NT
    safe_sin = np.where(offset == 0, 1.0, np.sin(angle))
    parity = np.where(offset % 2 == 0, 1.0, -1.0)
    deriv = np.where(offset == 0, 0.0, 0.5 * parity * np.cos(angle) / safe_sin)
    dspec = deriv + 2.0 / NT
    table = np.zeros((NT, 16), np.float64)
    for s in range(NT):
        y, x, c = s // 8, (s // 2) % 4, s % 2
        members = [s, s ^ 1, s ^ 8, s ^ 9]
        targets = [y * 8 + column * 2 + c for column in range(4)]
        table[s] = [dspec[m, t] for t in targets for m in members]
    return table.astype(np.float32)


def mix_kernel(index_ref, coef_ref, own_ref, mate_ref, across_ref, diagonal_ref, o_ref):
    me = index_ref[0]
    coef = [[coef_ref[me, slot * 4 + m] for m in range(4)] for slot in range(4)]
    chunk = 32

    def step(c, carry):
        rows = pl.ds(pl.multiple_of(c * chunk, chunk), chunk)
        values = (own_ref[rows, :], mate_ref[rows, :], across_ref[rows, :], diagonal_ref[rows, :])
        for slot in range(4):
            acc = coef[slot][0] * values[0]
            for m in range(1, 4):
                acc = acc + coef[slot][m] * values[m]
            o_ref[slot, rows, :] = acc
        return carry

    lax.fori_loop(0, own_ref.shape[0] // chunk, step, 0, unroll=True)


def partial_sums(index, own, mate, across, diagonal):
    rows, lanes = own.shape
    block = 128
    flat = pl.BlockSpec((block, lanes), lambda r, index: (r, 0))
    return pl.pallas_call(
        mix_kernel,
        grid_spec=pltpu.PrefetchScalarGridSpec(
            num_scalar_prefetch=1,
            grid=(rows // block,),
            in_specs=[pl.BlockSpec(memory_space=pltpu.SMEM), flat, flat, flat, flat],
            out_specs=pl.BlockSpec((4, block, lanes), lambda r, index: (0, r, 0)),
        ),
        out_shape=jax.ShapeDtypeStruct((4, rows, lanes), jnp.float32),
    )(index, jnp.asarray(coefficient_table()), own, mate, across, diagonal)


def update_kernel(got_ref, base_ref, scale_ref, cond_ref, lam_ref, *rest):
    rows, lanes = base_ref.shape
    groups = scale_ref.shape[0]
    spec = (got_ref[0] + got_ref[1]) + (got_ref[2] + got_ref[3])
    scale = jnp.broadcast_to(scale_ref[...][:, None, :], (groups, rows // groups, lanes)).reshape(rows, lanes)
    lam = base_ref[...] - scale * spec
    lam_ref[...] = lam
    for weighted_ref in rest:
        cond = jnp.broadcast_to(cond_ref[...][:, None, :], (groups, rows // groups, lanes)).reshape(rows, lanes)
        weighted_ref[...] = lam * cond


def updated(got, base, scale, cond, outputs):
    rows, lanes = base.shape
    block = 256
    groups = block * scale.shape[0] // rows
    flat = pl.BlockSpec((block, lanes), lambda r: (r, 0))
    narrow = pl.BlockSpec((groups, lanes), lambda r: (r, 0))
    return pl.pallas_call(
        update_kernel,
        grid=(rows // block,),
        in_specs=[pl.BlockSpec((4, block, lanes), lambda r: (0, r, 0)), flat, narrow, narrow],
        out_specs=[flat] * outputs,
        out_shape=[jax.ShapeDtypeStruct(base.shape, jnp.float32)] * outputs,
    )(got, base, scale, cond)


def instance_mix(flat):
    i = lax.axis_index("iy") * 8 + lax.axis_index("ix") * 2 + lax.axis_index("ic")
    mate = routed(flat, lambda s: s ^ 1)
    across = routed(flat, lambda s: s ^ 8)
    diagonal = routed(across, lambda s: s ^ 1)
    partials = partial_sums(jnp.reshape(i, (1,)).astype(jnp.int32), flat, mate, across, diagonal)
    return partials, lax.all_to_all(partials, "ix", 0, 0)


def shards(lam_init, rhs, relax, cond, jac, rotor_jac, cols, rotor_shift, owned):
    local_inst = lam_init.shape[0]
    rows = lam_init.shape[1]
    rotor_rows = rotor_jac.shape[1]
    shape = lam_init.shape
    lanes = shape[-1]
    row = jnp.arange(rows)
    live = ((row >= rows - rotor_rows) | (row < owned[0])).astype(jnp.float32)[None, :, None, None]
    lam = lam_init * live
    moving = rotor_shift.astype(jnp.float32)[:, :, None, None]
    relax_wide = relax[:, :, None, :]
    cond_wide = cond[None, :, None, :]
    scale = relax[0] * live[0, :, 0]
    weighted = (lam * cond_wide).reshape(-1, lanes)
    for sweep in range(SWEEPS):
        lam_b = lam.astype(jnp.bfloat16)
        partials, got = instance_mix(weighted)
        records = jnp.einsum(
            "tjri,tjio->tjro",
            lam_b[:, rows - rotor_rows :],
            rotor_jac,
            preferred_element_type=jnp.float32,
        )
        onward = jnp.concatenate([lam_b[:, rows - 1 :], (records * moving).astype(jnp.bfloat16)], axis=1)
        onward, lam_b, _ = lax.optimization_barrier((onward, lam_b, partials))
        onward = shifted(onward, "sector", 1)
        head = shifted(lam_b[:, :1], "sector", -1)
        lam_h = jnp.concatenate([onward[:, :1], lam_b, head], axis=1)
        picked = lam_h[:, cols]
        stator = jnp.einsum("tnkri,tnkio->tnro", picked, jac, preferred_element_type=jnp.float32)
        arrived = onward[:, 1:].astype(jnp.float32)
        rotor = records * (1.0 - moving) + arrived
        rotor_full = jnp.concatenate(
            [jnp.zeros((local_inst, rows - rotor_rows) + rotor.shape[2:], jnp.float32), rotor],
            axis=1,
        )
        base = lam + relax_wide * (rhs - (stator + rotor_full)) * live
        fresh = updated(got, base.reshape(-1, lanes), scale, cond, 2 if sweep + 1 < SWEEPS else 1)
        lam = fresh[0].reshape(shape)
        weighted = fresh[-1]
    return lam


def solution(mesh):
    fine = jax.sharding.Mesh(mesh.devices.reshape(2, 4, 2, -1), INST + ("sector",))
    return jax.shard_map(
        shards,
        mesh=fine,
        in_specs=(
            P(INST, "sector", None, None),
            P(INST, "sector", None, None),
            P(INST, "sector", None),
            P("sector", None),
            P(INST, "sector", None, None, None),
            P(INST, "sector", None, None),
            P("sector", None),
            P(INST, "sector"),
            P("sector"),
        ),
        out_specs=P(INST, "sector", None, None),
        check_vma=False,
    )
```

```python
import jax
import jax.numpy as jnp
import numpy as np
from jax.experimental import pallas as pl
from jax.experimental.pallas import tpu as pltpu
from jax import lax
from jax.sharding import PartitionSpec as P

NT = 16
SWEEPS = 2


def padded(cells, sides, width):
    for axis, dim in sides:
        count = lax.axis_size(axis)
        head = lax.slice_in_dim(cells, 0, width, axis=dim)
        tail = lax.slice_in_dim(cells, cells.shape[dim] - width, cells.shape[dim], axis=dim)
        cells = jnp.concatenate(
            [
                lax.ppermute(tail, axis, [(i, (i + 1) % count) for i in range(count)]),
                cells,
                lax.ppermute(head, axis, [((i + 1) % count, i) for i in range(count)]),
            ],
            axis=dim,
        )
    return cells


def shifted(block, axis, distance):
    devices = range(lax.axis_size(axis))
    route = [((i - distance) % len(devices), i) for i in devices]
    return lax.ppermute(block, axis, route)


def spectral_matrix():
    index = jnp.arange(NT)
    offset = index[:, None] - index[None, :]
    angle = jnp.pi * offset.astype(jnp.float32) / NT
    safe_sin = jnp.where(offset == 0, jnp.float32(1.0), jnp.sin(angle))
    parity = jnp.where(offset % 2 == 0, jnp.float32(1.0), jnp.float32(-1.0))
    deriv = jnp.where(offset == 0, jnp.float32(0.0), 0.5 * parity * jnp.cos(angle) / safe_sin)
    return deriv + jnp.float32(2.0) / NT


INST = ("iy", "ix", "ic")


def routed(block, dest):
    return lax.ppermute(block, INST, [(s, dest(s)) for s in range(NT)])


def coefficient_table():
    index = np.arange(NT)
    offset = index[:, None] - index[None, :]
    angle = np.pi * offset / NT
    safe_sin = np.where(offset == 0, 1.0, np.sin(angle))
    parity = np.where(offset % 2 == 0, 1.0, -1.0)
    deriv = np.where(offset == 0, 0.0, 0.5 * parity * np.cos(angle) / safe_sin)
    dspec = deriv + 2.0 / NT
    table = np.zeros((NT, 16), np.float64)
    for s in range(NT):
        y, x, c = s // 8, (s // 2) % 4, s % 2
        members = [s, s ^ 1, s ^ 8, s ^ 9]
        targets = [y * 8 + column * 2 + c for column in range(4)]
        table[s] = [dspec[m, t] for t in targets for m in members]
    return table.astype(np.float32)


def mix_kernel(index_ref, coef_ref, own_ref, mate_ref, across_ref, diagonal_ref, o_ref):
    me = index_ref[0]
    coef = [[coef_ref[me, slot * 4 + m] for m in range(4)] for slot in range(4)]
    chunk = 32

    def step(c, carry):
        rows = pl.ds(pl.multiple_of(c * chunk, chunk), chunk)
        values = (own_ref[rows, :], mate_ref[rows, :], across_ref[rows, :], diagonal_ref[rows, :])
        for slot in range(4):
            acc = coef[slot][0] * values[0]
            for m in range(1, 4):
                acc = acc + coef[slot][m] * values[m]
            o_ref[slot, rows, :] = acc
        return carry

    lax.fori_loop(0, own_ref.shape[0] // chunk, step, 0, unroll=True)


def partial_sums(index, own, mate, across, diagonal):
    rows, lanes = own.shape
    block = 256
    flat = pl.BlockSpec((block, lanes), lambda r, index: (r, 0))
    return pl.pallas_call(
        mix_kernel,
        grid_spec=pltpu.PrefetchScalarGridSpec(
            num_scalar_prefetch=1,
            grid=(rows // block,),
            in_specs=[pl.BlockSpec(memory_space=pltpu.SMEM), flat, flat, flat, flat],
            out_specs=pl.BlockSpec((4, block, lanes), lambda r, index: (0, r, 0)),
        ),
        out_shape=jax.ShapeDtypeStruct((4, rows, lanes), jnp.float32),
    )(index, jnp.asarray(coefficient_table()), own, mate, across, diagonal)


def update_kernel(got_ref, base_ref, scale_ref, cond_ref, lam_ref, *rest):
    rows, lanes = base_ref.shape
    groups = scale_ref.shape[0]
    spec = (got_ref[0] + got_ref[1]) + (got_ref[2] + got_ref[3])
    scale = jnp.broadcast_to(scale_ref[...][:, None, :], (groups, rows // groups, lanes)).reshape(rows, lanes)
    lam = base_ref[...] - scale * spec
    lam_ref[...] = lam
    if rest:
        cond = jnp.broadcast_to(cond_ref[...][:, None, :], (groups, rows // groups, lanes)).reshape(rows, lanes)
        rest[0][...] = lam * cond
        rest[1][...] = lam.astype(jnp.bfloat16)


def updated(got, base, scale, cond, outputs):
    rows, lanes = base.shape
    block = 256
    groups = block * scale.shape[0] // rows
    flat = pl.BlockSpec((block, lanes), lambda r: (r, 0))
    narrow = pl.BlockSpec((groups, lanes), lambda r: (r, 0))
    return pl.pallas_call(
        update_kernel,
        grid=(rows // block,),
        in_specs=[pl.BlockSpec((4, block, lanes), lambda r: (0, r, 0)), flat, narrow, narrow],
        out_specs=[flat] * outputs,
        out_shape=[jax.ShapeDtypeStruct(base.shape, jnp.float32)] * min(outputs, 2)
        + [jax.ShapeDtypeStruct(base.shape, jnp.bfloat16)] * (outputs - 2),
    )(got, base, scale, cond)


def instance_mix(flat):
    i = lax.axis_index("iy") * 8 + lax.axis_index("ix") * 2 + lax.axis_index("ic")
    mate = routed(flat, lambda s: s ^ 1)
    across = routed(flat, lambda s: s ^ 8)
    diagonal = routed(across, lambda s: s ^ 1)
    partials = partial_sums(jnp.reshape(i, (1,)).astype(jnp.int32), flat, mate, across, diagonal)
    return partials, lax.all_to_all(partials, "ix", 0, 0)


def shards(lam_init, rhs, relax, cond, jac, rotor_jac, cols, rotor_shift, owned):
    local_inst = lam_init.shape[0]
    rows = lam_init.shape[1]
    rotor_rows = rotor_jac.shape[1]
    shape = lam_init.shape
    lanes = shape[-1]
    row = jnp.arange(rows)
    live = ((row >= rows - rotor_rows) | (row < owned[0])).astype(jnp.float32)[None, :, None, None]
    lam = lam_init * live
    moving = rotor_shift.astype(jnp.float32)[:, :, None, None]
    relax_wide = relax[:, :, None, :]
    cond_wide = cond[None, :, None, :]
    scale = relax[0] * live[0, :, 0]
    weighted = (lam * cond_wide).reshape(-1, lanes)
    lam_b = lam.astype(jnp.bfloat16)
    for sweep in range(SWEEPS):
        partials, got = instance_mix(weighted)
        records = jnp.einsum(
            "tjri,tjio->tjro",
            lam_b[:, rows - rotor_rows :],
            rotor_jac,
            preferred_element_type=jnp.float32,
        )
        onward = jnp.concatenate([lam_b[:, rows - 1 :], (records * moving).astype(jnp.bfloat16)], axis=1)
        onward, lam_b, _ = lax.optimization_barrier((onward, lam_b, partials))
        onward = shifted(onward, "sector", 1)
        head = shifted(lam_b[:, :1], "sector", -1)
        lam_h = jnp.concatenate([onward[:, :1], lam_b, head], axis=1)
        picked = lam_h[:, cols]
        stator = jnp.einsum("tnkri,tnkio->tnro", picked, jac, preferred_element_type=jnp.float32)
        arrived = onward[:, 1:].astype(jnp.float32)
        rotor = records * (1.0 - moving) + arrived
        rotor_full = jnp.concatenate(
            [jnp.zeros((local_inst, rows - rotor_rows) + rotor.shape[2:], jnp.float32), rotor],
            axis=1,
        )
        base = lam + relax_wide * (rhs - (stator + rotor_full)) * live
        fresh = updated(got, base.reshape(-1, lanes), scale, cond, 3 if sweep + 1 < SWEEPS else 1)
        lam = fresh[0].reshape(shape)
        if len(fresh) > 1:
            weighted = fresh[1]
            lam_b = fresh[2].reshape(shape)
    return lam


def solution(mesh):
    fine = jax.sharding.Mesh(mesh.devices.reshape(2, 4, 2, -1), INST + ("sector",))
    return jax.shard_map(
        shards,
        mesh=fine,
        in_specs=(
            P(INST, "sector", None, None),
            P(INST, "sector", None, None),
            P(INST, "sector", None),
            P("sector", None),
            P(INST, "sector", None, None, None),
            P(INST, "sector", None, None),
            P("sector", None),
            P(INST, "sector"),
            P("sector"),
        ),
        out_specs=P(INST, "sector", None, None),
        check_vma=False,
    )
```

```python
import jax
import jax.numpy as jnp
import numpy as np
from jax.experimental import pallas as pl
from jax.experimental.pallas import tpu as pltpu
from jax import lax
from jax.sharding import PartitionSpec as P

NT = 16
SWEEPS = 2


def padded(cells, sides, width):
    for axis, dim in sides:
        count = lax.axis_size(axis)
        head = lax.slice_in_dim(cells, 0, width, axis=dim)
        tail = lax.slice_in_dim(cells, cells.shape[dim] - width, cells.shape[dim], axis=dim)
        cells = jnp.concatenate(
            [
                lax.ppermute(tail, axis, [(i, (i + 1) % count) for i in range(count)]),
                cells,
                lax.ppermute(head, axis, [((i + 1) % count, i) for i in range(count)]),
            ],
            axis=dim,
        )
    return cells


def shifted(block, axis, distance):
    devices = range(lax.axis_size(axis))
    route = [((i - distance) % len(devices), i) for i in devices]
    return lax.ppermute(block, axis, route)


def spectral_matrix():
    index = jnp.arange(NT)
    offset = index[:, None] - index[None, :]
    angle = jnp.pi * offset.astype(jnp.float32) / NT
    safe_sin = jnp.where(offset == 0, jnp.float32(1.0), jnp.sin(angle))
    parity = jnp.where(offset % 2 == 0, jnp.float32(1.0), jnp.float32(-1.0))
    deriv = jnp.where(offset == 0, jnp.float32(0.0), 0.5 * parity * jnp.cos(angle) / safe_sin)
    return deriv + jnp.float32(2.0) / NT


INST = ("iy", "ix", "ic")


def routed(block, dest):
    return lax.ppermute(block, INST, [(s, dest(s)) for s in range(NT)])


def coefficient_table():
    index = np.arange(NT)
    offset = index[:, None] - index[None, :]
    angle = np.pi * offset / NT
    safe_sin = np.where(offset == 0, 1.0, np.sin(angle))
    parity = np.where(offset % 2 == 0, 1.0, -1.0)
    deriv = np.where(offset == 0, 0.0, 0.5 * parity * np.cos(angle) / safe_sin)
    dspec = deriv + 2.0 / NT
    table = np.zeros((NT, 16), np.float64)
    for s in range(NT):
        y, x, c = s // 8, (s // 2) % 4, s % 2
        members = [s, s ^ 1, s ^ 8, s ^ 9]
        targets = [y * 8 + column * 2 + c for column in range(4)]
        table[s] = [dspec[m, t] for t in targets for m in members]
    return table.astype(np.float32)


def mix_kernel(index_ref, coef_ref, own_ref, mate_ref, across_ref, diagonal_ref, o_ref):
    me = index_ref[0]
    coef = [[coef_ref[me, slot * 4 + m] for m in range(4)] for slot in range(4)]
    chunk = 64

    def step(c, carry):
        rows = pl.ds(pl.multiple_of(c * chunk, chunk), chunk)
        values = (own_ref[rows, :], mate_ref[rows, :], across_ref[rows, :], diagonal_ref[rows, :])
        for slot in range(4):
            acc = coef[slot][0] * values[0]
            for m in range(1, 4):
                acc = acc + coef[slot][m] * values[m]
            o_ref[slot, rows, :] = acc
        return carry

    lax.fori_loop(0, own_ref.shape[0] // chunk, step, 0, unroll=True)


def partial_sums(index, own, mate, across, diagonal):
    rows, lanes = own.shape
    block = 256
    flat = pl.BlockSpec((block, lanes), lambda r, index: (r, 0))
    return pl.pallas_call(
        mix_kernel,
        grid_spec=pltpu.PrefetchScalarGridSpec(
            num_scalar_prefetch=1,
            grid=(rows // block,),
            in_specs=[pl.BlockSpec(memory_space=pltpu.SMEM), flat, flat, flat, flat],
            out_specs=pl.BlockSpec((4, block, lanes), lambda r, index: (0, r, 0)),
        ),
        out_shape=jax.ShapeDtypeStruct((4, rows, lanes), jnp.float32),
    )(index, jnp.asarray(coefficient_table()), own, mate, across, diagonal)


def update_kernel(got_ref, base_ref, scale_ref, cond_ref, lam_ref, *rest):
    rows, lanes = base_ref.shape
    groups = scale_ref.shape[0]
    spec = (got_ref[0] + got_ref[1]) + (got_ref[2] + got_ref[3])
    scale = jnp.broadcast_to(scale_ref[...][:, None, :], (groups, rows // groups, lanes)).reshape(rows, lanes)
    lam = base_ref[...] - scale * spec
    lam_ref[...] = lam
    for weighted_ref in rest:
        cond = jnp.broadcast_to(cond_ref[...][:, None, :], (groups, rows // groups, lanes)).reshape(rows, lanes)
        weighted_ref[...] = lam * cond


def updated(got, base, scale, cond, outputs):
    rows, lanes = base.shape
    block = 256
    groups = block * scale.shape[0] // rows
    flat = pl.BlockSpec((block, lanes), lambda r: (r, 0))
    narrow = pl.BlockSpec((groups, lanes), lambda r: (r, 0))
    return pl.pallas_call(
        update_kernel,
        grid=(rows // block,),
        in_specs=[pl.BlockSpec((4, block, lanes), lambda r: (0, r, 0)), flat, narrow, narrow],
        out_specs=[flat] * outputs,
        out_shape=[jax.ShapeDtypeStruct(base.shape, jnp.float32)] * outputs,
    )(got, base, scale, cond)


def instance_mix(flat):
    i = lax.axis_index("iy") * 8 + lax.axis_index("ix") * 2 + lax.axis_index("ic")
    mate = routed(flat, lambda s: s ^ 1)
    across = routed(flat, lambda s: s ^ 8)
    diagonal = routed(across, lambda s: s ^ 1)
    partials = partial_sums(jnp.reshape(i, (1,)).astype(jnp.int32), flat, mate, across, diagonal)
    return partials, lax.all_to_all(partials, "ix", 0, 0)


def shards(lam_init, rhs, relax, cond, jac, rotor_jac, cols, rotor_shift, owned):
    local_inst = lam_init.shape[0]
    rows = lam_init.shape[1]
    rotor_rows = rotor_jac.shape[1]
    shape = lam_init.shape
    lanes = shape[-1]
    row = jnp.arange(rows)
    live = ((row >= rows - rotor_rows) | (row < owned[0])).astype(jnp.float32)[None, :, None, None]
    lam = lam_init * live
    moving = rotor_shift.astype(jnp.float32)[:, :, None, None]
    relax_wide = relax[:, :, None, :]
    cond_wide = cond[None, :, None, :]
    scale = relax[0] * live[0, :, 0]
    weighted = (lam * cond_wide).reshape(-1, lanes)
    for sweep in range(SWEEPS):
        lam_b = lam.astype(jnp.bfloat16)
        partials, got = instance_mix(weighted)
        records = jnp.einsum(
            "tjri,tjio->tjro",
            lam_b[:, rows - rotor_rows :],
            rotor_jac,
            preferred_element_type=jnp.float32,
        )
        onward = jnp.concatenate([lam_b[:, rows - 1 :], (records * moving).astype(jnp.bfloat16)], axis=1)
        onward, lam_b, _ = lax.optimization_barrier((onward, lam_b, partials))
        onward = shifted(onward, "sector", 1)
        head = shifted(lam_b[:, :1], "sector", -1)
        lam_h = jnp.concatenate([onward[:, :1], lam_b, head], axis=1)
        picked = lam_h[:, cols]
        stator = jnp.einsum("tnkri,tnkio->tnro", picked, jac, preferred_element_type=jnp.float32)
        arrived = onward[:, 1:].astype(jnp.float32)
        rotor = records * (1.0 - moving) + arrived
        rotor_full = jnp.concatenate(
            [jnp.zeros((local_inst, rows - rotor_rows) + rotor.shape[2:], jnp.float32), rotor],
            axis=1,
        )
        base = lam + relax_wide * (rhs - (stator + rotor_full)) * live
        fresh = updated(got, base.reshape(-1, lanes), scale, cond, 2 if sweep + 1 < SWEEPS else 1)
        lam = fresh[0].reshape(shape)
        weighted = fresh[-1]
    return lam


def solution(mesh):
    fine = jax.sharding.Mesh(mesh.devices.reshape(2, 4, 2, -1), INST + ("sector",))
    return jax.shard_map(
        shards,
        mesh=fine,
        in_specs=(
            P(INST, "sector", None, None),
            P(INST, "sector", None, None),
            P(INST, "sector", None),
            P("sector", None),
            P(INST, "sector", None, None, None),
            P(INST, "sector", None, None),
            P("sector", None),
            P(INST, "sector"),
            P("sector"),
        ),
        out_specs=P(INST, "sector", None, None),
        check_vma=False,
    )
```

```python
import jax
import jax.numpy as jnp
import numpy as np
from jax.experimental import pallas as pl
from jax.experimental.pallas import tpu as pltpu
from jax import lax
from jax.sharding import PartitionSpec as P

NT = 16
SWEEPS = 2


def padded(cells, sides, width):
    for axis, dim in sides:
        count = lax.axis_size(axis)
        head = lax.slice_in_dim(cells, 0, width, axis=dim)
        tail = lax.slice_in_dim(cells, cells.shape[dim] - width, cells.shape[dim], axis=dim)
        cells = jnp.concatenate(
            [
                lax.ppermute(tail, axis, [(i, (i + 1) % count) for i in range(count)]),
                cells,
                lax.ppermute(head, axis, [((i + 1) % count, i) for i in range(count)]),
            ],
            axis=dim,
        )
    return cells


def shifted(block, axis, distance):
    devices = range(lax.axis_size(axis))
    route = [((i - distance) % len(devices), i) for i in devices]
    return lax.ppermute(block, axis, route)


def spectral_matrix():
    index = jnp.arange(NT)
    offset = index[:, None] - index[None, :]
    angle = jnp.pi * offset.astype(jnp.float32) / NT
    safe_sin = jnp.where(offset == 0, jnp.float32(1.0), jnp.sin(angle))
    parity = jnp.where(offset % 2 == 0, jnp.float32(1.0), jnp.float32(-1.0))
    deriv = jnp.where(offset == 0, jnp.float32(0.0), 0.5 * parity * jnp.cos(angle) / safe_sin)
    return deriv + jnp.float32(2.0) / NT


INST = ("iy", "ix", "ic")


def routed(block, dest):
    return lax.ppermute(block, INST, [(s, dest(s)) for s in range(NT)])


def coefficient_table():
    index = np.arange(NT)
    offset = index[:, None] - index[None, :]
    angle = np.pi * offset / NT
    safe_sin = np.where(offset == 0, 1.0, np.sin(angle))
    parity = np.where(offset % 2 == 0, 1.0, -1.0)
    deriv = np.where(offset == 0, 0.0, 0.5 * parity * np.cos(angle) / safe_sin)
    dspec = deriv + 2.0 / NT
    table = np.zeros((NT, 16), np.float64)
    for s in range(NT):
        y, x, c = s // 8, (s // 2) % 4, s % 2
        members = [s, s ^ 1, s ^ 8, s ^ 9]
        targets = [y * 8 + column * 2 + c for column in range(4)]
        table[s] = [dspec[m, t] for t in targets for m in members]
    return table.astype(np.float32)


def mix_kernel(index_ref, coef_ref, own_ref, mate_ref, across_ref, diagonal_ref, o_ref):
    me = index_ref[0]
    coef = [[coef_ref[me, slot * 4 + m] for m in range(4)] for slot in range(4)]
    chunk = 16

    def step(c, carry):
        rows = pl.ds(pl.multiple_of(c * chunk, chunk), chunk)
        values = (own_ref[rows, :], mate_ref[rows, :], across_ref[rows, :], diagonal_ref[rows, :])
        for slot in range(4):
            acc = coef[slot][0] * values[0]
            for m in range(1, 4):
                acc = acc + coef[slot][m] * values[m]
            o_ref[slot, rows, :] = acc
        return carry

    lax.fori_loop(0, own_ref.shape[0] // chunk, step, 0, unroll=True)


def partial_sums(index, own, mate, across, diagonal):
    rows, lanes = own.shape
    block = 256
    flat = pl.BlockSpec((block, lanes), lambda r, index: (r, 0))
    return pl.pallas_call(
        mix_kernel,
        grid_spec=pltpu.PrefetchScalarGridSpec(
            num_scalar_prefetch=1,
            grid=(rows // block,),
            in_specs=[pl.BlockSpec(memory_space=pltpu.SMEM), flat, flat, flat, flat],
            out_specs=pl.BlockSpec((4, block, lanes), lambda r, index: (0, r, 0)),
        ),
        out_shape=jax.ShapeDtypeStruct((4, rows, lanes), jnp.float32),
    )(index, jnp.asarray(coefficient_table()), own, mate, across, diagonal)


def update_kernel(got_ref, base_ref, scale_ref, cond_ref, lam_ref, *rest):
    rows, lanes = base_ref.shape
    groups = scale_ref.shape[0]
    spec = (got_ref[0] + got_ref[1]) + (got_ref[2] + got_ref[3])
    scale = jnp.broadcast_to(scale_ref[...][:, None, :], (groups, rows // groups, lanes)).reshape(rows, lanes)
    lam = base_ref[...] - scale * spec
    lam_ref[...] = lam
    for weighted_ref in rest:
        cond = jnp.broadcast_to(cond_ref[...][:, None, :], (groups, rows // groups, lanes)).reshape(rows, lanes)
        weighted_ref[...] = lam * cond


def updated(got, base, scale, cond, outputs):
    rows, lanes = base.shape
    block = 256
    groups = block * scale.shape[0] // rows
    flat = pl.BlockSpec((block, lanes), lambda r: (r, 0))
    narrow = pl.BlockSpec((groups, lanes), lambda r: (r, 0))
    return pl.pallas_call(
        update_kernel,
        grid=(rows // block,),
        in_specs=[pl.BlockSpec((4, block, lanes), lambda r: (0, r, 0)), flat, narrow, narrow],
        out_specs=[flat] * outputs,
        out_shape=[jax.ShapeDtypeStruct(base.shape, jnp.float32)] * outputs,
    )(got, base, scale, cond)


def instance_mix(flat):
    i = lax.axis_index("iy") * 8 + lax.axis_index("ix") * 2 + lax.axis_index("ic")
    mate = routed(flat, lambda s: s ^ 1)
    across = routed(flat, lambda s: s ^ 8)
    diagonal = routed(across, lambda s: s ^ 1)
    partials = partial_sums(jnp.reshape(i, (1,)).astype(jnp.int32), flat, mate, across, diagonal)
    return partials, lax.all_to_all(partials, "ix", 0, 0)


def shards(lam_init, rhs, relax, cond, jac, rotor_jac, cols, rotor_shift, owned):
    local_inst = lam_init.shape[0]
    rows = lam_init.shape[1]
    rotor_rows = rotor_jac.shape[1]
    shape = lam_init.shape
    lanes = shape[-1]
    row = jnp.arange(rows)
    live = ((row >= rows - rotor_rows) | (row < owned[0])).astype(jnp.float32)[None, :, None, None]
    lam = lam_init * live
    moving = rotor_shift.astype(jnp.float32)[:, :, None, None]
    relax_wide = relax[:, :, None, :]
    cond_wide = cond[None, :, None, :]
    scale = relax[0] * live[0, :, 0]
    weighted = (lam * cond_wide).reshape(-1, lanes)
    for sweep in range(SWEEPS):
        lam_b = lam.astype(jnp.bfloat16)
        partials, got = instance_mix(weighted)
        records = jnp.einsum(
            "tjri,tjio->tjro",
            lam_b[:, rows - rotor_rows :],
            rotor_jac,
            preferred_element_type=jnp.float32,
        )
        onward = jnp.concatenate([lam_b[:, rows - 1 :], (records * moving).astype(jnp.bfloat16)], axis=1)
        onward, lam_b, _ = lax.optimization_barrier((onward, lam_b, partials))
        onward = shifted(onward, "sector", 1)
        head = shifted(lam_b[:, :1], "sector", -1)
        lam_h = jnp.concatenate([onward[:, :1], lam_b, head], axis=1)
        picked = lam_h[:, cols]
        stator = jnp.einsum("tnkri,tnkio->tnro", picked, jac, preferred_element_type=jnp.float32)
        arrived = onward[:, 1:].astype(jnp.float32)
        rotor = records * (1.0 - moving) + arrived
        rotor_full = jnp.concatenate(
            [jnp.zeros((local_inst, rows - rotor_rows) + rotor.shape[2:], jnp.float32), rotor],
            axis=1,
        )
        base = lam + relax_wide * (rhs - (stator + rotor_full)) * live
        fresh = updated(got, base.reshape(-1, lanes), scale, cond, 2 if sweep + 1 < SWEEPS else 1)
        lam = fresh[0].reshape(shape)
        weighted = fresh[-1]
    return lam


def solution(mesh):
    fine = jax.sharding.Mesh(mesh.devices.reshape(2, 4, 2, -1), INST + ("sector",))
    return jax.shard_map(
        shards,
        mesh=fine,
        in_specs=(
            P(INST, "sector", None, None),
            P(INST, "sector", None, None),
            P(INST, "sector", None),
            P("sector", None),
            P(INST, "sector", None, None, None),
            P(INST, "sector", None, None),
            P("sector", None),
            P(INST, "sector"),
            P("sector"),
        ),
        out_specs=P(INST, "sector", None, None),
        check_vma=False,
    )
```
